32 devices in a mesh: gx: 8 (over z, x), yz: 4 (over y, core).
Axes of the slice: x: 2, y: 2, z: 4, core: 2. Of those that a mesh axis runs over, the one named last changes fastest.
Arguments:
- populations: float32 [19, 64, 32, 128], P(None, 'gx', 'yz'), may hold values from 0.02 to 0.1
- cell_grain: int32 [64, 32, 128], P('gx', 'yz'), may hold values from -1 to 1023, as said below
- near_rows: int32 [32, 1024], P(('gx', 'yz')), may hold values from -1 to 511, as said below
- contact_pairs: int32 [2, 32768], P(None, ('gx', 'yz')), may hold values from 0 to 1023, as said below
- grain_position: float32 [3, 16384], P(None, ('gx', 'yz')), may hold values from 0 to 6
- grain_velocity: float32 [3, 16384], P(None, ('gx', 'yz')), may hold values from -0.1 to 0.1
- grain_radius: float32 [16384], P(('gx', 'yz')), may hold values from 0.8 to 1.6
- grain_mass: float32 [16384], P(('gx', 'yz')), may hold values from 2 to 20
Outputs:
- populations_next: float32 [19, 64, 32, 128], P(None, 'gx', 'yz')
- velocity_next: float32 [3, 16384], P(None, ('gx', 'yz'))
- position_next: float32 [3, 16384], P(None, ('gx', 'yz'))
The draws below stay inside these ranges and needn't reach their ends.
Inputs may be any that keep to these rules, and one draw needn't show every extreme that they name: `near_rows`: entry o * 32 + s of device d's row names a row of device o's grains or is -1; in each block of 32 entries the live ones come first, are distinct, and number 1 to 32; every device has one block with all 32 live. `cell_grain`: A solid cell names a live entry of the list of the device whose brick holds it; the share of solid cells differs from brick to brick. `contact_pairs`: column p belongs to device p // 1024: its first row is a row of that device's grains, its second a live entry of that device's list.
All inputs are finite; a program needn't handle non-finite values.
Results may differ from the reference program's by a relative error of at most 0.0003.
Values sent between devices are 32-bit elements; how exact they have to be, the bound alone decides.
A program may use at most 64 MiB of HBM per device.

```python
import math
import jax
import jax.numpy as jnp
import numpy as np
from jax import lax

CX = 8
CY = 8
CZ = 128
GR_DEV = 512
NEAR = 1024
PAIRS_DEV = 1024
SLOT = 32
NX = 64
NY = 32
GRAINS = 16384
PAIRS = 32768
N_YZ = 4
DEVICES = 32


def grain_layout(key):
    base = jax.random.fold_in(key, 7)
    key_count, key_full, key_rows = jax.random.split(base, 3)
    counts = jax.random.randint(key_count, (DEVICES, DEVICES), 1, SLOT + 1)
    full = jax.random.randint(key_full, (DEVICES,), 0, DEVICES)
    counts = jnp.where(jnp.arange(DEVICES)[None, :] == full[:, None], SLOT, counts)
    return (counts.astype(jnp.int32), key_rows)


def live_entry(key, device, counts):
    key_owner, key_slot = jax.random.split(key)
    owner = jax.random.randint(key_owner, device.shape, 0, DEVICES)
    slot = jax.random.randint(key_slot, device.shape, 0, counts[device, owner])
    return (owner * SLOT + slot).astype(jnp.int32)


def draw_near_rows(key, part):
    counts, key_rows = grain_layout(key)
    scores = jax.random.randint(key_rows, (DEVICES, DEVICES, GR_DEV), 0, 2 ** 30 // GR_DEV)
    scores = scores * GR_DEV + jnp.arange(GR_DEV, dtype=jnp.int32)
    picked = lax.top_k(scores, SLOT)[1]
    slots = jnp.arange(SLOT, dtype=jnp.int32)
    rows = jnp.where(slots[None, None, :] < counts[:, :, None], picked, -1)
    return rows.reshape(DEVICES, NEAR).astype(jnp.int32)


def draw_cell_grain(key, part):
    counts, key_rows = grain_layout(key)
    base = jax.random.fold_in(key, 19)
    key_share, key_solid, key_entry = jax.random.split(base, 3)
    device = (jnp.arange(NX, dtype=jnp.int32) // CX)[:, None, None] * N_YZ + (jnp.arange(NY, dtype=jnp.int32) // CY)[None, :, None]
    device = jnp.broadcast_to(device, (NX, NY, CZ))
    share = jax.random.randint(key_share, (DEVICES,), 10, 61)
    solid = jax.random.randint(key_solid, (NX, NY, CZ), 0, 100) < share[device]
    entry = live_entry(key_entry, device, counts)
    return jnp.where(solid, entry, -1).astype(jnp.int32)


def draw_contact_pairs(key, part):
    counts, key_rows = grain_layout(key)
    base = jax.random.fold_in(key, 31)
    key_first, key_second = jax.random.split(base)
    device = jnp.arange(PAIRS, dtype=jnp.int32) // PAIRS_DEV
    first = jax.random.randint(key_first, (PAIRS,), 0, GR_DEV)
    second = live_entry(key_second, device, counts)
    return jnp.stack([first.astype(jnp.int32), second]).astype(jnp.int32)


def levels(stream_key, extent, cuts, low, top_value):
    gain = 1.0
    for axis_at, blocks in cuts:
        draws = jax.random.uniform(jax.random.fold_in(jax.random.fold_in(stream_key, 6), axis_at), (blocks,), jnp.float32, low / len(cuts), top_value / len(cuts))
        gain = gain * jnp.repeat(jnp.exp(draws), extent[axis_at] // blocks).reshape((-1,) + (1,) * (len(extent) - 1 - axis_at))
    return gain


def setup_inputs(seed: int = 0) -> dict:
    keys = jax.random.split(jax.random.key(seed), 9)
    populations = jnp.clip(0.02 + 0.08 * jax.random.uniform(keys[0], (19, NX, NY, CZ), jnp.float32) ** levels(keys[0], (19, NX, NY, CZ), ((1, 8), (2, 4)), -0.2, 0.2), 0.02, 0.1)
    cell_grain = draw_cell_grain(jax.random.fold_in(keys[8], 71), 0)
    near_rows = draw_near_rows(jax.random.fold_in(keys[8], 71), 0)
    contact_pairs = draw_contact_pairs(jax.random.fold_in(keys[8], 71), 0)
    grain_position = jnp.clip(6.0 * jax.random.uniform(keys[4], (3, GRAINS), jnp.float32) ** levels(keys[4], (3, GRAINS), ((1, 32),), -0.2, 0.2), 0.0, 6.0)
    grain_velocity = jnp.clip(jax.random.uniform(keys[5], (3, GRAINS), jnp.float32, -0.1, 0.1) * levels(keys[5], (3, GRAINS), ((1, 32),), -0.4, 0.0), -0.1, 0.1)
    grain_radius = jnp.clip(0.8 + 0.8 * jax.random.uniform(keys[6], (GRAINS,), jnp.float32) ** levels(keys[6], (GRAINS,), ((0, 32),), -0.2, 0.2), 0.8, 1.6)
    grain_mass = jnp.clip(jnp.exp(math.log(20.0) - 2.3025851 * jax.random.uniform(keys[7], (GRAINS,), jnp.float32) ** levels(keys[7], (GRAINS,), ((0, 32),), -0.2, 0.2)), 2.0, 20.0)
    return dict(populations=populations, cell_grain=cell_grain, near_rows=near_rows, contact_pairs=contact_pairs, grain_position=grain_position, grain_velocity=grain_velocity, grain_radius=grain_radius, grain_mass=grain_mass)


lattice_dirs = ((0, 0, 0), (1, 0, 0), (-1, 0, 0), (0, 1, 0), (0, -1, 0), (0, 0, 1), (0, 0, -1), (1, 1, 0), (-1, -1, 0), (1, -1, 0), (-1, 1, 0), (1, 0, 1), (-1, 0, -1), (1, 0, -1), (-1, 0, 1), (0, 1, 1), (0, -1, -1), (0, 1, -1), (0, -1, 1))
lattice_weights = (1.0 / 3.0,) + (1.0 / 18.0,) * 6 + (1.0 / 36.0,) * 12
opposite = (0, 2, 1, 4, 3, 6, 5, 8, 7, 10, 9, 12, 11, 14, 13, 16, 15, 18, 17)
relax_rate = 1.25
stiffness = 0.5
damping = 0.5

def project(direction, parts):
    total = None
    for compo in range(3):
        factor = lattice_dirs[direction][compo]
        if factor != 0:
            term = factor * parts[compo]
            total = term if total is None else total + term
    return total

def collide(populations):
    density = lax.optimization_barrier(jnp.sum(populations, axis=0))
    speeds = []
    for compo in range(3):
        moment = jnp.zeros_like(density)
        for direction in range(19):
            factor = lattice_dirs[direction][compo]
            if factor != 0:
                moment = moment + factor * populations[direction]
        speeds.append(moment / density)
    square = speeds[0] * speeds[0] + speeds[1] * speeds[1] + speeds[2] * speeds[2]
    result = []
    for direction in range(19):
        if direction == 0:
            equil = lattice_weights[0] * density * (1.0 - 1.5 * square)
        else:
            along = project(direction, speeds)
            equil = lattice_weights[direction] * density * (1.0 + 3.0 * along + 4.5 * along * along - 1.5 * square)
        result.append(populations[direction] + relax_rate * (equil - populations[direction]))
    return jnp.stack(result)

def stream_force(populations, fluid, pick):
    here = pick(list(range(24)), 0, 0, 0)
    fresh = [here[0]]
    force = [jnp.zeros_like(here[0]) for compo in range(3)]
    for direction in range(1, 19):
        shift_x, shift_y, shift_z = lattice_dirs[direction]
        back = opposite[direction]
        weight = lattice_weights[direction]
        source = pick([direction, 19, 20, 21, 22], shift_x, shift_y, shift_z)
        bounce = here[back] + 6.0 * weight * here[23] * project(direction, source[1:4])
        fresh.append(source[4] * source[0] + (1.0 - source[4]) * bounce)
        target = pick([back, 22, 23], -shift_x, -shift_y, -shift_z)
        link = target[1] * (2.0 * target[0] + 6.0 * weight * target[2] * project(direction, here[19:22])) * (1.0 - here[22])
        for compo in range(3):
            factor = lattice_dirs[direction][compo]
            if factor != 0:
                force[compo] = force[compo] - factor * link
    read = jnp.where(fluid[None], jnp.stack(fresh), populations)
    return (read, jnp.stack(force))

def contact_force(pos_a, vel_a, rad_a, pos_b, vel_b, rad_b):
    offset = pos_a - pos_b
    length = jnp.sqrt(lax.optimization_barrier(jnp.sum(offset * offset, axis=0)))
    normal = offset / jnp.maximum(length, 1.0)
    intersection = jnp.maximum(rad_a + rad_b - length, 0.0)
    closing = lax.optimization_barrier(jnp.sum((vel_a - vel_b) * normal, axis=0))
    return (stiffness * intersection - damping * intersection * closing) * normal

def reference(populations, cell_grain, near_rows, contact_pairs, grain_position, grain_velocity, grain_radius, grain_mass):
    slot_owner = jnp.arange(NEAR, dtype=jnp.int32) // SLOT
    near_grain = slot_owner[None, :] * GR_DEV + jnp.maximum(near_rows, 0)
    brick = (jnp.arange(NX, dtype=jnp.int32) // CX)[:, None, None] * N_YZ + (jnp.arange(NY, dtype=jnp.int32) // CY)[None, :, None]
    solid = cell_grain >= 0
    grain_cell = near_grain[brick, jnp.maximum(cell_grain, 0)]
    wall = grain_velocity[:, grain_cell] * solid.astype(jnp.float32)[None]
    post = collide(populations)
    table = jnp.concatenate([post, wall, (~solid).astype(jnp.float32)[None], lax.optimization_barrier(jnp.sum(post, axis=0))[None]], 0)

    def pick(channels, shift_x, shift_y, shift_z):
        return jnp.roll(table[np.array(channels)], (shift_x, shift_y, shift_z), axis=(1, 2, 3))
    read, cell_force = stream_force(populations, ~solid, pick)
    flat_ids = jnp.where(solid, grain_cell, GRAINS).reshape(-1).astype(jnp.int32)
    fluid_force = jax.ops.segment_sum(cell_force.reshape(3, -1).T, flat_ids, GRAINS + 1)[:GRAINS].T
    pair_dev = jnp.arange(PAIRS, dtype=jnp.int32) // PAIRS_DEV
    first = pair_dev * GR_DEV + contact_pairs[0]
    second = near_grain[pair_dev, contact_pairs[1]]
    push = contact_force(grain_position[:, first], grain_velocity[:, first], grain_radius[first], grain_position[:, second], grain_velocity[:, second], grain_radius[second])
    contact_total = jax.ops.segment_sum(push.T, first, GRAINS).T
    velocity_next = grain_velocity + (fluid_force + contact_total) / grain_mass[None]
    position_next = grain_position + velocity_next
    return (read, velocity_next, position_next)
```

```python
import functools

import jax
import jax.numpy as jnp
from jax import lax
from jax.experimental import pallas as pl
from jax.experimental.pallas import tpu as pltpu
from jax.sharding import PartitionSpec as P

lattice_dirs = (
    (0, 0, 0),
    (1, 0, 0),
    (-1, 0, 0),
    (0, 1, 0),
    (0, -1, 0),
    (0, 0, 1),
    (0, 0, -1),
    (1, 1, 0),
    (-1, -1, 0),
    (1, -1, 0),
    (-1, 1, 0),
    (1, 0, 1),
    (-1, 0, -1),
    (1, 0, -1),
    (-1, 0, 1),
    (0, 1, 1),
    (0, -1, -1),
    (0, 1, -1),
    (0, -1, 1),
)
lattice_weights = (1.0 / 3.0,) + (1.0 / 18.0,) * 6 + (1.0 / 36.0,) * 12
opposite = (0, 2, 1, 4, 3, 6, 5, 8, 7, 10, 9, 12, 11, 14, 13, 16, 15, 18, 17)
relax_rate = 1.25
stiffness = 0.5
damping = 0.5

still = (0, 3, 4, 5, 6, 15, 16, 17, 18)
ahead = (1, 7, 9, 11, 13)
behind = (2, 8, 10, 12, 14)
channel = {}
for place, name in enumerate(still + ahead):
    channel[name] = place
RHO = len(still) + len(ahead)
for place, name in enumerate(behind):
    channel[name] = RHO + 1 + place
CHANNELS = RHO + 1 + len(behind)
X_LOW = len(still)
rise = (3, 15, 17, 7, 19, 10)
fall = (4, 16, 18, 8, 19, 9)
channel[19] = RHO
FACE = 6
SUB = 8
LANE = 128


def project(direction, parts):
    total = None
    for compo in range(3):
        factor = lattice_dirs[direction][compo]
        if factor != 0:
            term = parts[compo] if factor > 0 else -parts[compo]
            total = term if total is None else total + term
    return total


def lookup(row, lanes):
    table = jnp.broadcast_to(row, lanes.shape)
    return jnp.take_along_axis(table, lanes, axis=1, mode="promise_in_bounds")


def lane_roll(value, shift):
    shift = shift % LANE
    return value if shift == 0 else pltpu.roll(value, shift, 1)


def sums_by_entry(parts, rows, lanes):
    sub = lax.broadcasted_iota(jnp.int32, (SUB, LANE), 0)
    tall = lax.broadcasted_iota(jnp.int32, (LANE, LANE), 0)
    left = [[] for part in parts]
    right = []
    for y in range(SUB):
        hit = jnp.broadcast_to(rows[y : y + 1], (SUB, LANE)) == sub
        for which, part in enumerate(parts):
            spread = jnp.broadcast_to(part[y : y + 1], (SUB, LANE))
            left[which].append(jnp.where(hit, spread, 0.0))
        match = jnp.broadcast_to(lanes[y : y + 1], (LANE, LANE)) == tall
        right.append(jnp.where(match, 1.0, 0.0).astype(jnp.bfloat16))
    wide = [jnp.concatenate(pieces, axis=1) for pieces in left]
    wide.append(jnp.zeros_like(wide[0]))
    full = jnp.concatenate(wide, axis=0)
    first = full.astype(jnp.bfloat16)
    rest = full - first.astype(jnp.float32)
    second = rest.astype(jnp.bfloat16)
    third = (rest - second.astype(jnp.float32)).astype(jnp.bfloat16)
    table = jnp.concatenate(right, axis=1)
    total = lax.dot_general(
        jnp.concatenate([first, second, third], axis=0),
        table,
        (((1,), (1,)), ((), ())),
        preferred_element_type=jnp.float32,
    )
    return total[0:32] + total[32:64] + total[64:96]


def contact_push(pos_a, vel_a, rad_a, pos_b, vel_b, rad_b):
    offset = [a - b for a, b in zip(pos_a, pos_b)]
    length = jnp.sqrt(offset[0] * offset[0] + offset[1] * offset[1] + offset[2] * offset[2])
    scale = jnp.maximum(length, 1.0)
    normal = [part / scale for part in offset]
    intersection = jnp.maximum(rad_a + rad_b - length, 0.0)
    closing = (
        (vel_a[0] - vel_b[0]) * normal[0]
        + (vel_a[1] - vel_b[1]) * normal[1]
        + (vel_a[2] - vel_b[2]) * normal[2]
    )
    amount = stiffness * intersection - damping * intersection * closing
    return [amount * part for part in normal]


def kernel(
    count_x,
    count_y,
    slot,
    pops,
    cells,
    near,
    pairs,
    position,
    velocity,
    radius,
    mass,
    out_pops,
    out_vel,
    out_pos,
    asked,
    reply,
    known,
    sent_force,
    got_force,
    table,
    wall,
    low_src,
    high_src,
    low_rows,
    high_rows,
    pair_ids,
    send_sems,
    recv_sems,
    halo_send,
    halo_recv,
):
    devices = count_x * count_y
    groups = devices // SUB
    per_row = LANE // slot
    width = pops.shape[1]
    owned = position.shape[1]
    banks = owned // LANE
    at_x = lax.axis_index("gx")
    at_y = lax.axis_index("yz")
    me = at_x * count_y + at_y
    sub = lax.broadcasted_iota(jnp.int32, (SUB, LANE), 0)
    lane = lax.broadcasted_iota(jnp.int32, (SUB, LANE), 1)

    def peer_of(step):
        peer = lax.rem(me + step, devices)
        return peer, (peer // count_y, lax.rem(peer, count_y))

    barrier = pltpu.get_barrier_semaphore()

    def greet(step, carry):
        peer, where = peer_of(step)
        pl.semaphore_signal(
            barrier, inc=1, device_id=where, device_id_type=pl.DeviceIdType.MESH
        )
        return carry

    lax.fori_loop(1, devices, greet, 0)
    asked[pl.ds(me, 1)] = near[pl.ds(me // per_row, 1)]
    pl.semaphore_wait(barrier, devices - 1)

    def everyone(source_of, target, which):
        def start(step, carry):
            peer, where = peer_of(step)
            pltpu.make_async_remote_copy(
                src_ref=source_of(peer),
                dst_ref=target.at[pl.ds(me, 1)],
                send_sem=send_sems.at[which],
                recv_sem=recv_sems.at[which],
                device_id=where,
                device_id_type=pl.DeviceIdType.MESH,
            ).start()
            return carry

        lax.fori_loop(1, devices, start, 0)

    def arrived(target, sems, which):
        part = target.at[pl.ds(0, devices - 1)]
        pltpu.make_async_copy(part, part, sems.at[which]).wait()

    everyone(lambda peer: near.at[pl.ds(peer // per_row, 1)], asked, 0)

    def collide(x, carry):
        values = [pops[i, x] for i in range(19)]
        density = values[0]
        for i in range(1, 19):
            density = density + values[i]
        scale = 1.0 / density
        speeds = []
        for compo in range(3):
            moment = None
            for i in range(19):
                factor = lattice_dirs[i][compo]
                if factor != 0:
                    if moment is None:
                        moment = values[i]
                    elif factor > 0:
                        moment = moment + values[i]
                    else:
                        moment = moment - values[i]
            speeds.append(moment * scale)
        square = speeds[0] * speeds[0] + speeds[1] * speeds[1] + speeds[2] * speeds[2]
        base = 1.0 - 1.5 * square
        weighted = {w: (relax_rate * w) * density for w in set(lattice_weights)}
        keep = 1.0 - relax_rate
        fresh = keep * values[0] + weighted[lattice_weights[0]] * base
        table[channel[0], x + 1] = fresh
        after = fresh
        for i in range(1, 19, 2):
            along = project(i, speeds)
            even = base + 4.5 * along * along
            odd = 3.0 * along
            gain = weighted[lattice_weights[i]]
            plus = keep * values[i] + gain * (even + odd)
            minus = keep * values[i + 1] + gain * (even - odd)
            table[channel[i], x + 1] = plus
            table[channel[i + 1], x + 1] = minus
            after = after + plus + minus
        table[RHO, x + 1] = jnp.where(cells[x] >= 0, 0.0, after)
        return carry

    lax.fori_loop(0, width, collide, 0)

    arrived(asked, recv_sems, 0)
    quarter = lax.rem(me, per_row)
    field = lane // slot
    within = lane - field * slot
    wanted = []
    for q in range(groups):
        ask = asked[q * SUB : (q + 1) * SUB, 0, :]
        row = jnp.take_along_axis(
            ask, within + quarter * slot, axis=1, mode="promise_in_bounds"
        )
        wanted.append(row)
        safe = jnp.maximum(row, 0)
        bank = safe // LANE
        spot = safe - bank * LANE
        vel_row = jnp.zeros((SUB, LANE), jnp.float32)
        pos_row = jnp.zeros((SUB, LANE), jnp.float32)
        for h in range(banks):
            span = slice(h * LANE, (h + 1) * LANE)
            for compo in range(3):
                mine = (bank == h) & (field == compo)
                vel_row = jnp.where(mine, lookup(velocity[compo : compo + 1, span], spot), vel_row)
                pos_row = jnp.where(mine, lookup(position[compo : compo + 1, span], spot), pos_row)
            mine = (bank == h) & (field == 3)
            pos_row = jnp.where(mine, lookup(radius[0:1, span], spot), pos_row)
        reply[q * SUB : (q + 1) * SUB, 0, :] = vel_row
        reply[q * SUB : (q + 1) * SUB, 1, :] = pos_row
    everyone(lambda peer: reply.at[pl.ds(peer, 1)], known, 1)

    part_of_lane = lane // slot

    def to_table(read, compo):
        value = jnp.zeros((SUB, LANE), jnp.float32)
        for q in range(groups):
            moved = lane_roll(read(q), (q - compo) * slot)
            value = jnp.where(part_of_lane == q, moved, value)
        return value

    wanted_table = jnp.zeros((SUB, LANE), jnp.int32)
    for q in range(groups):
        wanted_table = jnp.where(part_of_lane == q, lane_roll(wanted[q], q * slot), wanted_table)
    wanted_bank = wanted_table // LANE
    wanted_bank = jnp.where(wanted_table < 0, SUB, wanted_bank)
    wanted_spot = jnp.bitwise_and(wanted_table, LANE - 1)

    arrived(known, recv_sems, 1)
    known[pl.ds(me, 1)] = reply[pl.ds(me, 1)]
    vel_table = [
        to_table(lambda q: known[q * SUB : (q + 1) * SUB, 0, :], compo) for compo in range(3)
    ]
    vel_rows = [[part[r : r + 1] for r in range(SUB)] for part in vel_table]

    def entry(ids):
        owner = ids // slot
        inner = ids - owner * slot
        row = jnp.bitwise_and(owner, SUB - 1)
        return row, (owner // SUB) * slot + inner

    def from_table(rows_of, row, spot):
        value = jnp.zeros((SUB, LANE), jnp.float32)
        for r in range(SUB):
            value = jnp.where(row == r, lookup(rows_of[r], spot), value)
        return value

    def fill_walls(x, carry):
        ids = cells[x]
        solid = ids >= 0
        row, spot = entry(jnp.maximum(ids, 0))
        speeds = [from_table(rows_of, row, spot) for rows_of in vel_rows]
        for compo in range(3):
            wall[compo, x] = speeds[compo]
        for i in range(1, 19, 2):
            motion = (6.0 * lattice_weights[i]) * project(i, speeds)
            plus = jnp.where(solid, motion, table[channel[i], x + 1])
            minus = jnp.where(solid, -motion, table[channel[i + 1], x + 1])
            table[channel[i], x + 1] = plus
            table[channel[i + 1], x + 1] = minus
            for which, value in ((i, plus), (i + 1, minus)):
                if which in rise:
                    high_src[rise.index(which), pl.ds(x, 1)] = value[SUB - 1 : SUB][None]
                if which in fall:
                    low_src[fall.index(which), pl.ds(x, 1)] = value[0:1][None]
        rho = table[RHO, x + 1]
        high_src[4, pl.ds(x, 1)] = rho[SUB - 1 : SUB][None]
        low_src[4, pl.ds(x, 1)] = rho[0:1][None]
        return carry

    lax.fori_loop(0, width, fill_walls, 0)

    right = lax.rem(at_x + 1, count_x)
    left = lax.rem(at_x + count_x - 1, count_x)
    upper = lax.rem(at_y + 1, count_y)
    lower = lax.rem(at_y + count_y - 1, count_y)
    end = width - 1
    hops = (
        (table.at[X_LOW : X_LOW + FACE, width], table.at[X_LOW : X_LOW + FACE, 0], right, at_y),
        (table.at[RHO : RHO + FACE, 1], table.at[RHO : RHO + FACE, width + 1], left, at_y),
        (high_src, low_rows.at[:, 1 : width + 1], at_x, upper),
        (low_src, high_rows.at[:, 1 : width + 1], at_x, lower),
        (high_src.at[3:5, end], low_rows.at[3:5, 0], right, upper),
        (high_src.at[4:6, 0], low_rows.at[4:6, width + 1], left, upper),
        (low_src.at[3:5, 0], high_rows.at[3:5, width + 1], left, lower),
        (low_src.at[4:6, end], high_rows.at[4:6, 0], right, lower),
    )
    copies = []
    for which, (source, target, to_x, to_y) in enumerate(hops):
        copy = pltpu.make_async_remote_copy(
            src_ref=source,
            dst_ref=target,
            send_sem=halo_send.at[which],
            recv_sem=halo_recv.at[which],
            device_id=(to_x, to_y),
            device_id_type=pl.DeviceIdType.MESH,
        )
        copy.start()
        copies.append(copy)

    for y in range(SUB):
        pair_ids[0, y : y + 1] = pairs[0:1, y * LANE : (y + 1) * LANE]
        pair_ids[1, y : y + 1] = pairs[1:2, y * LANE : (y + 1) * LANE]
    first = pair_ids[0]
    first_bank = first // LANE
    first_spot = first - first_bank * LANE

    def from_owned(ref, compo):
        value = jnp.zeros((SUB, LANE), jnp.float32)
        for h in range(banks):
            part = lookup(ref[compo : compo + 1, h * LANE : (h + 1) * LANE], first_spot)
            value = jnp.where(first_bank == h, part, value)
        return value

    row, spot = entry(pair_ids[1])

    def from_known(field_table):
        return from_table([field_table[r : r + 1] for r in range(SUB)], row, spot)

    pos_table = [
        to_table(lambda q: known[q * SUB : (q + 1) * SUB, 1, :], compo) for compo in range(4)
    ]
    push = contact_push(
        [from_owned(position, compo) for compo in range(3)],
        [from_owned(velocity, compo) for compo in range(3)],
        from_owned(radius, 0),
        [from_known(pos_table[compo]) for compo in range(3)],
        [from_known(vel_table[compo]) for compo in range(3)],
        from_known(pos_table[3]),
    )
    contact = sums_by_entry(push, first_bank, first_spot)

    for copy in copies:
        copy.wait()

    def stream(x, total):
        solid = cells[x] >= 0
        here_rho = table[RHO, x + 1]
        speeds = [wall[compo, x] for compo in range(3)]
        out_pops[0, x] = jnp.where(solid, pops[0, x], table[channel[0], x + 1])
        rows_made = {}

        def moved(name, shift_x, shift_y, shift_z):
            key = (name, shift_x, shift_y, 0)
            at = x + 1 - shift_x
            if key not in rows_made:
                value = table[channel[name], at]
                if shift_y > 0:
                    edge = jnp.broadcast_to(low_rows[rise.index(name), at], (SUB, LANE))
                    value = jnp.where(sub == 0, edge, pltpu.roll(value, 1, 0))
                elif shift_y < 0:
                    edge = jnp.broadcast_to(high_rows[fall.index(name), at], (SUB, LANE))
                    value = jnp.where(sub == SUB - 1, edge, pltpu.roll(value, SUB - 1, 0))
                rows_made[key] = value
            if shift_z == 0:
                return rows_made[key]
            deep = (name, shift_x, shift_y, shift_z)
            if deep not in rows_made:
                rows_made[deep] = lane_roll(rows_made[key], shift_z)
            return rows_made[deep]

        force = [jnp.zeros((SUB, LANE), jnp.float32) for compo in range(3)]
        for i in range(1, 19):
            shift = lattice_dirs[i]
            source = moved(i, *shift)
            rho = moved(19, *shift)
            fluid = rho > 0.0
            bounce = table[channel[opposite[i]], x + 1] + here_rho * source
            fresh = jnp.where(fluid, source, bounce)
            out_pops[i, x] = jnp.where(solid, pops[i, x], fresh)
            drag = rho * ((6.0 * lattice_weights[i]) * project(i, speeds))
            link = jnp.where(fluid, 2.0 * source - drag, 0.0)
            for compo in range(3):
                if shift[compo] > 0:
                    force[compo] = force[compo] + link
                elif shift[compo] < 0:
                    force[compo] = force[compo] - link
        force = [jnp.where(solid, part, 0.0) for part in force]
        where = entry(jnp.maximum(cells[x], 0))
        return total + sums_by_entry(force, *where)

    slot_force = lax.fori_loop(0, width, stream, jnp.zeros((32, LANE), jnp.float32))

    for q in range(groups):
        value = jnp.zeros((SUB, LANE), jnp.float32)
        for compo in range(3):
            part = lane_roll(slot_force[compo * SUB : (compo + 1) * SUB], (compo - q) * slot)
            value = jnp.where(field == compo, part, value)
        sent_force[q * SUB : (q + 1) * SUB, 0, :] = value
    everyone(lambda peer: sent_force.at[pl.ds(peer, 1)], got_force, 2)
    arrived(asked, send_sems, 0)
    arrived(reply, send_sems, 1)
    arrived(got_force, recv_sems, 2)
    got_force[pl.ds(me, 1)] = sent_force[pl.ds(me, 1)]
    gained = [
        to_table(lambda q: got_force[q * SUB : (q + 1) * SUB, 0, :], compo) for compo in range(3)
    ]
    fluid_force = sums_by_entry(gained, wanted_bank, wanted_spot)
    force = fluid_force + contact
    for compo in range(3):
        for h in range(banks):
            span = slice(h * LANE, (h + 1) * LANE)
            line = compo * SUB + h
            speed = velocity[compo : compo + 1, span] + force[line : line + 1] / mass[0:1, span]
            out_vel[compo : compo + 1, span] = speed
            out_pos[compo : compo + 1, span] = position[compo : compo + 1, span] + speed
    arrived(sent_force, send_sems, 2)


def local(
    populations,
    cell_grain,
    near_rows,
    contact_pairs,
    grain_position,
    grain_velocity,
    grain_radius,
    grain_mass,
):
    count_x = lax.axis_size("gx")
    count_y = lax.axis_size("yz")
    devices = count_x * count_y
    near_count = near_rows.shape[1]
    slot = near_count // devices
    owned = grain_position.shape[1]
    width = populations.shape[1]
    near_lines = near_rows.reshape(near_count // LANE, 1, LANE)
    whole = pl.BlockSpec(memory_space=pltpu.VMEM)
    f32 = jnp.float32
    return pl.pallas_call(
        functools.partial(kernel, count_x, count_y, slot),
        out_shape=(
            jax.ShapeDtypeStruct(populations.shape, f32),
            jax.ShapeDtypeStruct(grain_velocity.shape, f32),
            jax.ShapeDtypeStruct(grain_position.shape, f32),
        ),
        in_specs=[whole] * 8,
        out_specs=(whole,) * 3,
        scratch_shapes=[
            pltpu.VMEM((devices, 1, LANE), jnp.int32),
            pltpu.VMEM((devices, 2, LANE), f32),
            pltpu.VMEM((devices, 2, LANE), f32),
            pltpu.VMEM((devices, 1, LANE), f32),
            pltpu.VMEM((devices, 1, LANE), f32),
            pltpu.VMEM((CHANNELS, width + 2, SUB, LANE), f32),
            pltpu.VMEM((3, width, SUB, LANE), f32),
            pltpu.VMEM((FACE, width, 1, LANE), f32),
            pltpu.VMEM((FACE, width, 1, LANE), f32),
            pltpu.VMEM((FACE, width + 2, 1, LANE), f32),
            pltpu.VMEM((FACE, width + 2, 1, LANE), f32),
            pltpu.VMEM((2, SUB, LANE), jnp.int32),
            pltpu.SemaphoreType.DMA((3,)),
            pltpu.SemaphoreType.DMA((3,)),
            pltpu.SemaphoreType.DMA((8,)),
            pltpu.SemaphoreType.DMA((8,)),
        ],
        compiler_params=pltpu.CompilerParams(collective_id=0, has_side_effects=True),
        name="step",
    )(
        populations,
        cell_grain,
        near_lines,
        contact_pairs,
        grain_position,
        grain_velocity,
        grain_radius.reshape(1, owned),
        grain_mass.reshape(1, owned),
    )


def solution(mesh):
    return jax.shard_map(
        local,
        mesh=mesh,
        in_specs=(
            P(None, "gx", "yz", None),
            P("gx", "yz", None),
            P(("gx", "yz"), None),
            P(None, ("gx", "yz")),
            P(None, ("gx", "yz")),
            P(None, ("gx", "yz")),
            P(("gx", "yz")),
            P(("gx", "yz")),
        ),
        out_specs=(P(None, "gx", "yz", None), P(None, ("gx", "yz")), P(None, ("gx", "yz"))),
        check_vma=False,
    )
```

```python
import functools

import jax
import jax.numpy as jnp
from jax import lax
from jax.experimental import pallas as pl
from jax.experimental.pallas import tpu as pltpu
from jax.sharding import PartitionSpec as P

lattice_dirs = (
    (0, 0, 0),
    (1, 0, 0),
    (-1, 0, 0),
    (0, 1, 0),
    (0, -1, 0),
    (0, 0, 1),
    (0, 0, -1),
    (1, 1, 0),
    (-1, -1, 0),
    (1, -1, 0),
    (-1, 1, 0),
    (1, 0, 1),
    (-1, 0, -1),
    (1, 0, -1),
    (-1, 0, 1),
    (0, 1, 1),
    (0, -1, -1),
    (0, 1, -1),
    (0, -1, 1),
)
lattice_weights = (1.0 / 3.0,) + (1.0 / 18.0,) * 6 + (1.0 / 36.0,) * 12
opposite = (0, 2, 1, 4, 3, 6, 5, 8, 7, 10, 9, 12, 11, 14, 13, 16, 15, 18, 17)
relax_rate = 1.25
stiffness = 0.5
damping = 0.5

still = (0, 3, 4, 5, 6, 15, 16, 17, 18)
ahead = (1, 7, 9, 11, 13)
behind = (2, 8, 10, 12, 14)
channel = {}
for place, name in enumerate(still + ahead):
    channel[name] = place
RHO = len(still) + len(ahead)
for place, name in enumerate(behind):
    channel[name] = RHO + 1 + place
CHANNELS = RHO + 1 + len(behind)
X_LOW = len(still)
rise = (3, 15, 17, 7, 19, 10)
fall = (4, 16, 18, 8, 19, 9)
channel[19] = RHO
FACE = 6
SUB = 8
LANE = 128


def project(direction, parts):
    total = None
    for compo in range(3):
        factor = lattice_dirs[direction][compo]
        if factor != 0:
            term = parts[compo] if factor > 0 else -parts[compo]
            total = term if total is None else total + term
    return total


def lookup(row, lanes):
    table = jnp.broadcast_to(row, lanes.shape)
    return jnp.take_along_axis(table, lanes, axis=1, mode="promise_in_bounds")


def split(ids):
    return lax.shift_right_arithmetic(ids, 7), jnp.bitwise_and(ids, LANE - 1)


def lane_roll(value, shift):
    shift = shift % LANE
    return value if shift == 0 else pltpu.roll(value, shift, 1)


def sums_by_entry(parts, rows, lanes):
    sub = lax.broadcasted_iota(jnp.int32, (SUB, LANE), 0)
    tall = lax.broadcasted_iota(jnp.int32, (LANE, LANE), 0)
    left = [[] for part in parts]
    right = []
    for y in range(SUB):
        hit = jnp.broadcast_to(rows[y : y + 1], (SUB, LANE)) == sub
        for which, part in enumerate(parts):
            spread = jnp.broadcast_to(part[y : y + 1], (SUB, LANE))
            left[which].append(jnp.where(hit, spread, 0.0))
        match = jnp.broadcast_to(lanes[y : y + 1], (LANE, LANE)) == tall
        right.append(jnp.where(match, 1.0, 0.0).astype(jnp.bfloat16))
    wide = [jnp.concatenate(pieces, axis=1) for pieces in left]
    wide.append(jnp.zeros_like(wide[0]))
    full = jnp.concatenate(wide, axis=0)
    first = full.astype(jnp.bfloat16)
    rest = full - first.astype(jnp.float32)
    second = rest.astype(jnp.bfloat16)
    third = (rest - second.astype(jnp.float32)).astype(jnp.bfloat16)
    table = jnp.concatenate(right, axis=1)
    total = lax.dot_general(
        jnp.concatenate([first, second, third], axis=0),
        table,
        (((1,), (1,)), ((), ())),
        preferred_element_type=jnp.float32,
    )
    return total[0:32] + total[32:64] + total[64:96]


def contact_push(pos_a, vel_a, rad_a, pos_b, vel_b, rad_b):
    offset = [a - b for a, b in zip(pos_a, pos_b)]
    length = jnp.sqrt(offset[0] * offset[0] + offset[1] * offset[1] + offset[2] * offset[2])
    scale = jnp.maximum(length, 1.0)
    normal = [part / scale for part in offset]
    intersection = jnp.maximum(rad_a + rad_b - length, 0.0)
    closing = (
        (vel_a[0] - vel_b[0]) * normal[0]
        + (vel_a[1] - vel_b[1]) * normal[1]
        + (vel_a[2] - vel_b[2]) * normal[2]
    )
    amount = stiffness * intersection - damping * intersection * closing
    return [amount * part for part in normal]


def kernel(
    count_x,
    count_y,
    slot,
    pops_in,
    cells_in,
    near_in,
    pairs_in,
    position_in,
    velocity_in,
    radius_in,
    out_pops,
    out_force,
    pops,
    cells,
    near,
    pairs,
    position,
    velocity,
    radius,
    asked,
    reply,
    known,
    sent_force,
    got_force,
    table,
    wall,
    low_src,
    high_src,
    low_rows,
    high_rows,
    pair_ids,
    send_sems,
    recv_sems,
    halo_send,
    halo_recv,
    load_sems,
):
    devices = count_x * count_y
    groups = devices // SUB
    per_row = LANE // slot
    width = pops.shape[1]
    owned = position.shape[1]
    banks = owned // LANE
    at_x = lax.axis_index("gx")
    at_y = lax.axis_index("yz")
    me = at_x * count_y + at_y
    sub = lax.broadcasted_iota(jnp.int32, (SUB, LANE), 0)
    lane = lax.broadcasted_iota(jnp.int32, (SUB, LANE), 1)

    offsets = [
        (step_x, step_y)
        for step_x in sorted(range(count_x), key=lambda step: abs(2 * step - count_x))
        for step_y in reversed(range(count_y))
        if step_x or step_y
    ]
    line_x = [lax.rem(at_x + step, count_x) for step in range(count_x)]
    line_y = [lax.rem(at_y + step, count_y) for step in range(count_y)]

    barrier = pltpu.get_barrier_semaphore()
    for step_x, step_y in offsets:
        pl.semaphore_signal(
            barrier,
            inc=1,
            device_id=(line_x[step_x], line_y[step_y]),
            device_id_type=pl.DeviceIdType.MESH,
        )
    loads = []
    for place, (source, target) in enumerate(
        (
            (near_in, near),
            (velocity_in, velocity),
            (position_in, position),
            (radius_in, radius),
            (pops_in, pops),
            (cells_in, cells),
            (pairs_in, pairs),
        )
    ):
        load = pltpu.make_async_copy(source, target, load_sems.at[place])
        load.start()
        loads.append(load)
    loads[0].wait()
    asked[pl.ds(me, 1)] = near[pl.ds(me // per_row, 1)]
    pl.semaphore_wait(barrier, devices - 1)

    def everyone(source_of, target, which):
        for step_x, step_y in offsets:
            to_x, to_y = line_x[step_x], line_y[step_y]
            pltpu.make_async_remote_copy(
                src_ref=source_of(to_x * count_y + to_y),
                dst_ref=target.at[pl.ds(me, 1)],
                send_sem=send_sems.at[which],
                recv_sem=recv_sems.at[which],
                device_id=(to_x, to_y),
                device_id_type=pl.DeviceIdType.MESH,
            ).start()

    def arrived(target, sems, which):
        part = target.at[pl.ds(0, devices - 1)]
        pltpu.make_async_copy(part, part, sems.at[which]).wait()

    everyone(lambda peer: near.at[pl.ds(peer // per_row, 1)], asked, 0)
    for load in loads[1:]:
        load.wait()

    def collide(x, carry):
        values = [pops[i, x] for i in range(19)]
        density = values[0]
        for i in range(1, 19):
            density = density + values[i]
        scale = 1.0 / density
        speeds = []
        for compo in range(3):
            moment = None
            for i in range(19):
                factor = lattice_dirs[i][compo]
                if factor != 0:
                    if moment is None:
                        moment = values[i]
                    elif factor > 0:
                        moment = moment + values[i]
                    else:
                        moment = moment - values[i]
            speeds.append(moment * scale)
        square = speeds[0] * speeds[0] + speeds[1] * speeds[1] + speeds[2] * speeds[2]
        base = 1.0 - 1.5 * square
        weighted = {w: (relax_rate * w) * density for w in set(lattice_weights)}
        keep = 1.0 - relax_rate
        fresh = keep * values[0] + weighted[lattice_weights[0]] * base
        table[channel[0], x + 1] = fresh
        after = fresh
        for i in range(1, 19, 2):
            along = project(i, speeds)
            even = base + 4.5 * along * along
            odd = 3.0 * along
            gain = weighted[lattice_weights[i]]
            plus = keep * values[i] + gain * (even + odd)
            minus = keep * values[i + 1] + gain * (even - odd)
            table[channel[i], x + 1] = plus
            table[channel[i + 1], x + 1] = minus
            after = after + plus + minus
        table[RHO, x + 1] = jnp.where(cells[x] >= 0, 0.0, after)
        return carry

    lax.fori_loop(0, width, collide, 0)

    arrived(asked, recv_sems, 0)
    quarter = lax.rem(me, per_row)
    slot_bits = slot.bit_length() - 1
    field = lax.shift_right_logical(lane, slot_bits)
    within = jnp.bitwise_and(lane, slot - 1)
    wanted = []
    for q in range(groups):
        ask = asked[q * SUB : (q + 1) * SUB, 0, :]
        row = jnp.take_along_axis(
            ask, within + quarter * slot, axis=1, mode="promise_in_bounds"
        )
        wanted.append(row)
        safe = jnp.maximum(row, 0)
        bank, spot = split(safe)
        vel_row = jnp.zeros((SUB, LANE), jnp.float32)
        pos_row = jnp.zeros((SUB, LANE), jnp.float32)
        for h in range(banks):
            span = slice(h * LANE, (h + 1) * LANE)
            for compo in range(3):
                mine = (bank == h) & (field == compo)
                vel_row = jnp.where(mine, lookup(velocity[compo : compo + 1, span], spot), vel_row)
                pos_row = jnp.where(mine, lookup(position[compo : compo + 1, span], spot), pos_row)
            mine = (bank == h) & (field == 3)
            pos_row = jnp.where(mine, lookup(radius[0:1, span], spot), pos_row)
        reply[q * SUB : (q + 1) * SUB, 0, :] = vel_row
        reply[q * SUB : (q + 1) * SUB, 1, :] = pos_row
    everyone(lambda peer: reply.at[pl.ds(peer, 1)], known, 1)

    part_of_lane = field

    def to_table(read, compo):
        value = jnp.zeros((SUB, LANE), jnp.float32)
        for q in range(groups):
            moved = lane_roll(read(q), (q - compo) * slot)
            value = jnp.where(part_of_lane == q, moved, value)
        return value

    wanted_table = jnp.zeros((SUB, LANE), jnp.int32)
    for q in range(groups):
        wanted_table = jnp.where(part_of_lane == q, lane_roll(wanted[q], q * slot), wanted_table)
    wanted_bank, wanted_spot = split(wanted_table)

    arrived(known, recv_sems, 1)
    known[pl.ds(me, 1)] = reply[pl.ds(me, 1)]
    vel_table = [
        to_table(lambda q: known[q * SUB : (q + 1) * SUB, 0, :], compo) for compo in range(3)
    ]
    vel_rows = [[part[r : r + 1] for r in range(SUB)] for part in vel_table]

    def entry(ids):
        row = jnp.bitwise_and(lax.shift_right_logical(ids, slot_bits), SUB - 1)
        part = lax.shift_right_logical(ids, slot_bits + 3)
        inner = jnp.bitwise_and(ids, slot - 1)
        return row, jnp.bitwise_and(lax.shift_left(part, slot_bits) + inner, LANE - 1)

    def from_table(rows_of, row, spot):
        value = jnp.zeros((SUB, LANE), jnp.float32)
        for r in range(SUB):
            value = jnp.where(row == r, lookup(rows_of[r], spot), value)
        return value

    def fill_walls(x, carry):
        ids = cells[x]
        solid = ids >= 0
        row, spot = entry(ids)
        speeds = [from_table(rows_of, row, spot) for rows_of in vel_rows]
        for compo in range(3):
            wall[compo, x] = speeds[compo]
        for i in range(1, 19, 2):
            motion = (6.0 * lattice_weights[i]) * project(i, speeds)
            plus = jnp.where(solid, motion, table[channel[i], x + 1])
            minus = jnp.where(solid, -motion, table[channel[i + 1], x + 1])
            table[channel[i], x + 1] = plus
            table[channel[i + 1], x + 1] = minus
            for which, value in ((i, plus), (i + 1, minus)):
                if which in rise:
                    high_src[rise.index(which), pl.ds(x, 1)] = value[SUB - 1 : SUB][None]
                if which in fall:
                    low_src[fall.index(which), pl.ds(x, 1)] = value[0:1][None]
        rho = table[RHO, x + 1]
        high_src[4, pl.ds(x, 1)] = rho[SUB - 1 : SUB][None]
        low_src[4, pl.ds(x, 1)] = rho[0:1][None]
        return carry

    lax.fori_loop(0, width, fill_walls, 0)

    right = lax.rem(at_x + 1, count_x)
    left = lax.rem(at_x + count_x - 1, count_x)
    upper = lax.rem(at_y + 1, count_y)
    lower = lax.rem(at_y + count_y - 1, count_y)
    end = width - 1
    hops = (
        (table.at[X_LOW : X_LOW + FACE, width], table.at[X_LOW : X_LOW + FACE, 0], right, at_y),
        (table.at[RHO : RHO + FACE, 1], table.at[RHO : RHO + FACE, width + 1], left, at_y),
        (high_src, low_rows.at[:, 1 : width + 1], at_x, upper),
        (low_src, high_rows.at[:, 1 : width + 1], at_x, lower),
        (high_src.at[3:5, end], low_rows.at[3:5, 0], right, upper),
        (high_src.at[4:6, 0], low_rows.at[4:6, width + 1], left, upper),
        (low_src.at[3:5, 0], high_rows.at[3:5, width + 1], left, lower),
        (low_src.at[4:6, end], high_rows.at[4:6, 0], right, lower),
    )
    copies = []
    for which, (source, target, to_x, to_y) in enumerate(hops):
        copy = pltpu.make_async_remote_copy(
            src_ref=source,
            dst_ref=target,
            send_sem=halo_send.at[which],
            recv_sem=halo_recv.at[which],
            device_id=(to_x, to_y),
            device_id_type=pl.DeviceIdType.MESH,
        )
        copy.start()
        copies.append(copy)

    for y in range(SUB):
        pair_ids[0, y : y + 1] = pairs[0:1, y * LANE : (y + 1) * LANE]
        pair_ids[1, y : y + 1] = pairs[1:2, y * LANE : (y + 1) * LANE]
    first = pair_ids[0]
    first_bank, first_spot = split(first)

    def from_owned(ref, compo):
        value = jnp.zeros((SUB, LANE), jnp.float32)
        for h in range(banks):
            part = lookup(ref[compo : compo + 1, h * LANE : (h + 1) * LANE], first_spot)
            value = jnp.where(first_bank == h, part, value)
        return value

    row, spot = entry(pair_ids[1])

    def from_known(field_table):
        return from_table([field_table[r : r + 1] for r in range(SUB)], row, spot)

    pos_table = [
        to_table(lambda q: known[q * SUB : (q + 1) * SUB, 1, :], compo) for compo in range(4)
    ]
    push = contact_push(
        [from_owned(position, compo) for compo in range(3)],
        [from_owned(velocity, compo) for compo in range(3)],
        from_owned(radius, 0),
        [from_known(pos_table[compo]) for compo in range(3)],
        [from_known(vel_table[compo]) for compo in range(3)],
        from_known(pos_table[3]),
    )
    contact = sums_by_entry(push, first_bank, first_spot)

    for copy in copies:
        copy.wait()

    def stream(x, total):
        solid = cells[x] >= 0
        here_rho = table[RHO, x + 1]
        speeds = [wall[compo, x] for compo in range(3)]
        out_pops[0, x] = jnp.where(solid, pops[0, x], table[channel[0], x + 1])
        rows_made = {}

        def moved(name, shift_x, shift_y, shift_z):
            key = (name, shift_x, shift_y, 0)
            at = x + 1 - shift_x
            if key not in rows_made:
                value = table[channel[name], at]
                if shift_y > 0:
                    edge = jnp.broadcast_to(low_rows[rise.index(name), at], (SUB, LANE))
                    value = jnp.where(sub == 0, edge, pltpu.roll(value, 1, 0))
                elif shift_y < 0:
                    edge = jnp.broadcast_to(high_rows[fall.index(name), at], (SUB, LANE))
                    value = jnp.where(sub == SUB - 1, edge, pltpu.roll(value, SUB - 1, 0))
                rows_made[key] = value
            if shift_z == 0:
                return rows_made[key]
            deep = (name, shift_x, shift_y, shift_z)
            if deep not in rows_made:
                rows_made[deep] = lane_roll(rows_made[key], shift_z)
            return rows_made[deep]

        force = [jnp.zeros((SUB, LANE), jnp.float32) for compo in range(3)]
        for i in range(1, 19):
            shift = lattice_dirs[i]
            source = moved(i, *shift)
            rho = moved(19, *shift)
            fluid = rho > 0.0
            bounce = table[channel[opposite[i]], x + 1] + here_rho * source
            fresh = jnp.where(fluid, source, bounce)
            out_pops[i, x] = jnp.where(solid, pops[i, x], fresh)
            drag = rho * ((6.0 * lattice_weights[i]) * project(i, speeds))
            link = jnp.where(fluid, 2.0 * source - drag, 0.0)
            for compo in range(3):
                if shift[compo] > 0:
                    force[compo] = force[compo] + link
                elif shift[compo] < 0:
                    force[compo] = force[compo] - link
        force = [jnp.where(solid, part, 0.0) for part in force]
        where = entry(cells[x])
        return total + sums_by_entry(force, *where)

    slot_force = lax.fori_loop(0, width, stream, jnp.zeros((32, LANE), jnp.float32))

    for q in range(groups):
        value = jnp.zeros((SUB, LANE), jnp.float32)
        for compo in range(3):
            part = lane_roll(slot_force[compo * SUB : (compo + 1) * SUB], (compo - q) * slot)
            value = jnp.where(field == compo, part, value)
        sent_force[q * SUB : (q + 1) * SUB, 0, :] = value
    everyone(lambda peer: sent_force.at[pl.ds(peer, 1)], got_force, 2)
    arrived(asked, send_sems, 0)
    arrived(reply, send_sems, 1)
    arrived(got_force, recv_sems, 2)
    got_force[pl.ds(me, 1)] = sent_force[pl.ds(me, 1)]
    gained = [
        to_table(lambda q: got_force[q * SUB : (q + 1) * SUB, 0, :], compo) for compo in range(3)
    ]
    fluid_force = sums_by_entry(gained, wanted_bank, wanted_spot)
    force = fluid_force + contact
    for compo in range(3):
        for h in range(banks):
            span = slice(h * LANE, (h + 1) * LANE)
            line = compo * SUB + h
            out_force[compo : compo + 1, span] = force[line : line + 1]
    arrived(sent_force, send_sems, 2)


def local(
    populations,
    cell_grain,
    near_rows,
    contact_pairs,
    grain_position,
    grain_velocity,
    grain_radius,
    grain_mass,
):
    count_x = lax.axis_size("gx")
    count_y = lax.axis_size("yz")
    devices = count_x * count_y
    near_count = near_rows.shape[1]
    slot = near_count // devices
    owned = grain_position.shape[1]
    width = populations.shape[1]
    near_lines = near_rows.reshape(near_count // LANE, 1, LANE)
    whole = pl.BlockSpec(memory_space=pltpu.VMEM)
    f32 = jnp.float32
    assert slot & (slot - 1) == 0 and near_count == SUB * LANE
    radius_line = grain_radius.reshape(1, owned)
    read, force = pl.pallas_call(
        functools.partial(kernel, count_x, count_y, slot),
        out_shape=(
            pltpu.VMEM(populations.shape, f32),
            jax.ShapeDtypeStruct(grain_velocity.shape, f32),
        ),
        in_specs=[pl.BlockSpec(memory_space=pltpu.HBM)] * 7,
        out_specs=(whole,) * 2,
        scratch_shapes=[
            pltpu.VMEM(populations.shape, f32),
            pltpu.VMEM(cell_grain.shape, jnp.int32),
            pltpu.VMEM(near_lines.shape, jnp.int32),
            pltpu.VMEM(contact_pairs.shape, jnp.int32),
            pltpu.VMEM(grain_position.shape, f32),
            pltpu.VMEM(grain_velocity.shape, f32),
            pltpu.VMEM(radius_line.shape, f32),
            pltpu.VMEM((devices, 1, LANE), jnp.int32),
            pltpu.VMEM((devices, 2, LANE), f32),
            pltpu.VMEM((devices, 2, LANE), f32),
            pltpu.VMEM((devices, 1, LANE), f32),
            pltpu.VMEM((devices, 1, LANE), f32),
            pltpu.VMEM((CHANNELS, width + 2, SUB, LANE), f32),
            pltpu.VMEM((3, width, SUB, LANE), f32),
            pltpu.VMEM((FACE, width, 1, LANE), f32),
            pltpu.VMEM((FACE, width, 1, LANE), f32),
            pltpu.VMEM((FACE, width + 2, 1, LANE), f32),
            pltpu.VMEM((FACE, width + 2, 1, LANE), f32),
            pltpu.VMEM((2, SUB, LANE), jnp.int32),
            pltpu.SemaphoreType.DMA((3,)),
            pltpu.SemaphoreType.DMA((3,)),
            pltpu.SemaphoreType.DMA((8,)),
            pltpu.SemaphoreType.DMA((8,)),
            pltpu.SemaphoreType.DMA((7,)),
        ],
        compiler_params=pltpu.CompilerParams(
            collective_id=0, has_side_effects=True, vmem_limit_bytes=24 << 20
        ),
        name="step",
    )(
        *(
            pltpu.with_memory_space_constraint(array, pltpu.HBM)
            for array in (
                populations,
                cell_grain,
                near_lines,
                contact_pairs,
                grain_position,
                grain_velocity,
                radius_line,
            )
        )
    )
    velocity_next = grain_velocity + force / grain_mass[None]
    return read, velocity_next, grain_position + velocity_next


def solution(mesh):
    return jax.shard_map(
        local,
        mesh=mesh,
        in_specs=(
            P(None, "gx", "yz", None),
            P("gx", "yz", None),
            P(("gx", "yz"), None),
            P(None, ("gx", "yz")),
            P(None, ("gx", "yz")),
            P(None, ("gx", "yz")),
            P(("gx", "yz")),
            P(("gx", "yz")),
        ),
        out_specs=(P(None, "gx", "yz", None), P(None, ("gx", "yz")), P(None, ("gx", "yz"))),
        check_vma=False,
    )
```

```python
import functools

import jax
import jax.numpy as jnp
from jax import lax
from jax.experimental import pallas as pl
from jax.experimental.pallas import tpu as pltpu
from jax.sharding import PartitionSpec as P

lattice_dirs = (
    (0, 0, 0),
    (1, 0, 0),
    (-1, 0, 0),
    (0, 1, 0),
    (0, -1, 0),
    (0, 0, 1),
    (0, 0, -1),
    (1, 1, 0),
    (-1, -1, 0),
    (1, -1, 0),
    (-1, 1, 0),
    (1, 0, 1),
    (-1, 0, -1),
    (1, 0, -1),
    (-1, 0, 1),
    (0, 1, 1),
    (0, -1, -1),
    (0, 1, -1),
    (0, -1, 1),
)
lattice_weights = (1.0 / 3.0,) + (1.0 / 18.0,) * 6 + (1.0 / 36.0,) * 12
opposite = (0, 2, 1, 4, 3, 6, 5, 8, 7, 10, 9, 12, 11, 14, 13, 16, 15, 18, 17)
relax_rate = 1.25
stiffness = 0.5
damping = 0.5

still = (0, 3, 4, 5, 6, 15, 16, 17, 18)
ahead = (1, 7, 9, 11, 13)
behind = (2, 8, 10, 12, 14)
channel = {}
for place, name in enumerate(still + ahead):
    channel[name] = place
RHO = len(still) + len(ahead)
for place, name in enumerate(behind):
    channel[name] = RHO + 1 + place
CHANNELS = RHO + 1 + len(behind)
X_LOW = len(still)
rise = (3, 15, 17, 7, 19, 10)
fall = (4, 16, 18, 8, 19, 9)
channel[19] = RHO
FACE = 6
SUB = 8
LANE = 128


def project(direction, parts):
    total = None
    for compo in range(3):
        factor = lattice_dirs[direction][compo]
        if factor != 0:
            term = parts[compo] if factor > 0 else -parts[compo]
            total = term if total is None else total + term
    return total


def lookup(row, lanes):
    table = jnp.broadcast_to(row, lanes.shape)
    return jnp.take_along_axis(table, lanes, axis=1, mode="promise_in_bounds")


def split(ids):
    return lax.shift_right_arithmetic(ids, 7), jnp.bitwise_and(ids, LANE - 1)


def lane_roll(value, shift):
    shift = shift % LANE
    return value if shift == 0 else pltpu.roll(value, shift, 1)


def sums_by_entry(parts, rows, lanes):
    sub = lax.broadcasted_iota(jnp.int32, (SUB, LANE), 0)
    tall = lax.broadcasted_iota(jnp.int32, (LANE, LANE), 0)
    left = [[] for part in parts]
    right = []
    for y in range(SUB):
        hit = jnp.broadcast_to(rows[y : y + 1], (SUB, LANE)) == sub
        for which, part in enumerate(parts):
            spread = jnp.broadcast_to(part[y : y + 1], (SUB, LANE))
            left[which].append(jnp.where(hit, spread, 0.0))
        match = jnp.broadcast_to(lanes[y : y + 1], (LANE, LANE)) == tall
        right.append(jnp.where(match, 1.0, 0.0).astype(jnp.bfloat16))
    wide = [jnp.concatenate(pieces, axis=1) for pieces in left]
    wide.append(jnp.zeros_like(wide[0]))
    full = jnp.concatenate(wide, axis=0)
    first = full.astype(jnp.bfloat16)
    rest = full - first.astype(jnp.float32)
    second = rest.astype(jnp.bfloat16)
    third = (rest - second.astype(jnp.float32)).astype(jnp.bfloat16)
    table = jnp.concatenate(right, axis=1)
    total = lax.dot_general(
        jnp.concatenate([first, second, third], axis=0),
        table,
        (((1,), (1,)), ((), ())),
        preferred_element_type=jnp.float32,
    )
    return total[0:32] + total[32:64] + total[64:96]


def contact_push(pos_a, vel_a, rad_a, pos_b, vel_b, rad_b):
    offset = [a - b for a, b in zip(pos_a, pos_b)]
    length = jnp.sqrt(offset[0] * offset[0] + offset[1] * offset[1] + offset[2] * offset[2])
    scale = jnp.maximum(length, 1.0)
    normal = [part / scale for part in offset]
    intersection = jnp.maximum(rad_a + rad_b - length, 0.0)
    closing = (
        (vel_a[0] - vel_b[0]) * normal[0]
        + (vel_a[1] - vel_b[1]) * normal[1]
        + (vel_a[2] - vel_b[2]) * normal[2]
    )
    amount = stiffness * intersection - damping * intersection * closing
    return [amount * part for part in normal]


def kernel(
    count_x,
    count_y,
    slot,
    pops_in,
    cells_in,
    near_in,
    pairs_in,
    position_in,
    velocity_in,
    radius_in,
    out_pops,
    out_force,
    pops,
    cells,
    near,
    pairs,
    position,
    velocity,
    radius,
    vel_lines,
    all_vel,
    measure_vel,
    asked,
    reply,
    known,
    sent_force,
    got_force,
    table,
    wall,
    low_src,
    high_src,
    low_rows,
    high_rows,
    pair_ids,
    send_sems,
    recv_sems,
    halo_send,
    halo_recv,
    load_sems,
):
    devices = count_x * count_y
    groups = devices // SUB
    per_row = LANE // slot
    width = pops.shape[1]
    owned = position.shape[1]
    banks = owned // LANE
    at_x = lax.axis_index("gx")
    at_y = lax.axis_index("yz")
    me = at_x * count_y + at_y
    sub = lax.broadcasted_iota(jnp.int32, (SUB, LANE), 0)
    lane = lax.broadcasted_iota(jnp.int32, (SUB, LANE), 1)

    offsets = [
        (step_x, step_y)
        for step_x in sorted(range(count_x), key=lambda step: abs(2 * step - count_x))
        for step_y in reversed(range(count_y))
        if step_x or step_y
    ]
    line_x = [lax.rem(at_x + step, count_x) for step in range(count_x)]
    line_y = [lax.rem(at_y + step, count_y) for step in range(count_y)]

    barrier = pltpu.get_barrier_semaphore()
    for step_x, step_y in offsets:
        pl.semaphore_signal(
            barrier,
            inc=1,
            device_id=(line_x[step_x], line_y[step_y]),
            device_id_type=pl.DeviceIdType.MESH,
        )
    loads = []
    for place, (source, target) in enumerate(
        (
            (near_in, near),
            (velocity_in, velocity),
            (position_in, position),
            (radius_in, radius),
            (pops_in, pops),
            (cells_in, cells),
            (pairs_in, pairs),
        )
    ):
        load = pltpu.make_async_copy(source, target, load_sems.at[place])
        load.start()
        loads.append(load)
    my_line = me // per_row
    my_place = lax.rem(me, per_row)
    loads[1].wait()
    for compo in range(3):
        for h in range(banks):
            line = velocity[compo : compo + 1, h * LANE : (h + 1) * LANE]
            vel_lines[compo * banks + h] = line
            all_vel[my_place, compo * banks + h, my_line] = line
    loads[0].wait()
    asked[pl.ds(me, 1)] = near[pl.ds(me // per_row, 1)]
    pl.semaphore_wait(barrier, devices - 1)

    def everyone(source_of, target_at_me, which):
        for step_x, step_y in offsets:
            to_x, to_y = line_x[step_x], line_y[step_y]
            pltpu.make_async_remote_copy(
                src_ref=source_of(to_x * count_y + to_y),
                dst_ref=target_at_me,
                send_sem=send_sems.at[which],
                recv_sem=recv_sems.at[which],
                device_id=(to_x, to_y),
                device_id_type=pl.DeviceIdType.MESH,
            ).start()

    def arrived(target, sems, which):
        part = target if target is measure_vel else target.at[pl.ds(0, devices - 1)]
        pltpu.make_async_copy(part, part, sems.at[which]).wait()

    everyone(lambda peer: vel_lines, all_vel.at[my_place, :, my_line], 3)
    everyone(lambda peer: near.at[peer // per_row], asked.at[me], 0)
    for load in loads[2:]:
        load.wait()

    def collide(x, carry):
        values = [pops[i, x] for i in range(19)]
        density = values[0]
        for i in range(1, 19):
            density = density + values[i]
        scale = 1.0 / density
        speeds = []
        for compo in range(3):
            moment = None
            for i in range(19):
                factor = lattice_dirs[i][compo]
                if factor != 0:
                    if moment is None:
                        moment = values[i]
                    elif factor > 0:
                        moment = moment + values[i]
                    else:
                        moment = moment - values[i]
            speeds.append(moment * scale)
        square = speeds[0] * speeds[0] + speeds[1] * speeds[1] + speeds[2] * speeds[2]
        base = 1.0 - 1.5 * square
        weighted = {w: (relax_rate * w) * density for w in set(lattice_weights)}
        keep = 1.0 - relax_rate
        fresh = keep * values[0] + weighted[lattice_weights[0]] * base
        table[channel[0], x + 1] = fresh
        after = fresh
        for i in range(1, 19, 2):
            along = project(i, speeds)
            even = base + 4.5 * along * along
            odd = 3.0 * along
            gain = weighted[lattice_weights[i]]
            plus = keep * values[i] + gain * (even + odd)
            minus = keep * values[i + 1] + gain * (even - odd)
            table[channel[i], x + 1] = plus
            table[channel[i + 1], x + 1] = minus
            after = after + plus + minus
        table[RHO, x + 1] = jnp.where(cells[x] >= 0, 0.0, after)
        return carry

    lax.fori_loop(0, width, collide, 0)

    slot_bits = slot.bit_length() - 1
    field = lax.shift_right_logical(lane, slot_bits)
    near_bank, near_spot = split(
        jnp.concatenate([near[line] for line in range(SUB)], axis=0)
    )
    arrived(measure_vel, recv_sems, 3)
    vel_table = [jnp.zeros((SUB, LANE), jnp.float32) for compo in range(3)]
    for place in range(per_row):
        for h in range(banks):
            mine = (field == place) & (near_bank == h)
            for compo in range(3):
                lines = all_vel[place, compo * banks + h, :, 0, :]
                part = jnp.take_along_axis(
                    lines, near_spot, axis=1, mode="promise_in_bounds"
                )
                vel_table[compo] = jnp.where(mine, part, vel_table[compo])
    vel_rows = [[part[r : r + 1] for r in range(SUB)] for part in vel_table]

    def from_table(rows_of, row, spot):
        value = jnp.zeros((SUB, LANE), jnp.float32)
        for r in range(SUB):
            value = jnp.where(row == r, lookup(rows_of[r], spot), value)
        return value

    def fill_walls(x, carry):
        ids = cells[x]
        solid = ids >= 0
        row, spot = split(ids)
        speeds = [from_table(rows_of, row, spot) for rows_of in vel_rows]
        for compo in range(3):
            wall[compo, x] = speeds[compo]
        for i in range(1, 19, 2):
            motion = (6.0 * lattice_weights[i]) * project(i, speeds)
            plus = jnp.where(solid, motion, table[channel[i], x + 1])
            minus = jnp.where(solid, -motion, table[channel[i + 1], x + 1])
            table[channel[i], x + 1] = plus
            table[channel[i + 1], x + 1] = minus
            for which, value in ((i, plus), (i + 1, minus)):
                if which in rise:
                    high_src[rise.index(which), pl.ds(x, 1)] = value[SUB - 1 : SUB][None]
                if which in fall:
                    low_src[fall.index(which), pl.ds(x, 1)] = value[0:1][None]
        rho = table[RHO, x + 1]
        high_src[4, pl.ds(x, 1)] = rho[SUB - 1 : SUB][None]
        low_src[4, pl.ds(x, 1)] = rho[0:1][None]
        return carry

    lax.fori_loop(0, width, fill_walls, 0)

    right = lax.rem(at_x + 1, count_x)
    left = lax.rem(at_x + count_x - 1, count_x)
    upper = lax.rem(at_y + 1, count_y)
    lower = lax.rem(at_y + count_y - 1, count_y)
    end = width - 1
    hops = (
        (table.at[X_LOW : X_LOW + FACE, width], table.at[X_LOW : X_LOW + FACE, 0], right, at_y),
        (table.at[RHO : RHO + FACE, 1], table.at[RHO : RHO + FACE, width + 1], left, at_y),
        (high_src, low_rows.at[:, 1 : width + 1], at_x, upper),
        (low_src, high_rows.at[:, 1 : width + 1], at_x, lower),
        (high_src.at[3:5, end], low_rows.at[3:5, 0], right, upper),
        (high_src.at[4:6, 0], low_rows.at[4:6, width + 1], left, upper),
        (low_src.at[3:5, 0], high_rows.at[3:5, width + 1], left, lower),
        (low_src.at[4:6, end], high_rows.at[4:6, 0], right, lower),
    )
    copies = []
    for which, (source, target, to_x, to_y) in enumerate(hops):
        copy = pltpu.make_async_remote_copy(
            src_ref=source,
            dst_ref=target,
            send_sem=halo_send.at[which],
            recv_sem=halo_recv.at[which],
            device_id=(to_x, to_y),
            device_id_type=pl.DeviceIdType.MESH,
        )
        copy.start()
        copies.append(copy)

    arrived(asked, recv_sems, 0)
    quarter = my_place
    within = jnp.bitwise_and(lane, slot - 1)
    wanted = []
    for q in range(groups):
        ask = asked[q * SUB : (q + 1) * SUB, 0, :]
        row = jnp.take_along_axis(
            ask, within + quarter * slot, axis=1, mode="promise_in_bounds"
        )
        wanted.append(row)
        bank, spot = split(jnp.maximum(row, 0))
        pos_row = jnp.zeros((SUB, LANE), jnp.float32)
        for h in range(banks):
            span = slice(h * LANE, (h + 1) * LANE)
            for compo in range(4):
                source = radius[0:1, span] if compo == 3 else position[compo : compo + 1, span]
                mine = (bank == h) & (field == compo)
                pos_row = jnp.where(mine, lookup(source, spot), pos_row)
        reply[q * SUB : (q + 1) * SUB, 0, :] = pos_row
    everyone(lambda peer: reply.at[peer], known.at[my_place, my_line], 1)

    wanted_table = jnp.zeros((SUB, LANE), jnp.int32)
    for q in range(groups):
        wanted_table = jnp.where(field == q, lane_roll(wanted[q], q * slot), wanted_table)
    wanted_bank, wanted_spot = split(wanted_table)

    for copy in copies:
        copy.wait()

    def stream(x, total):
        solid = cells[x] >= 0
        here_rho = table[RHO, x + 1]
        speeds = [wall[compo, x] for compo in range(3)]
        out_pops[0, x] = jnp.where(solid, pops[0, x], table[channel[0], x + 1])
        rows_made = {}

        def moved(name, shift_x, shift_y, shift_z):
            key = (name, shift_x, shift_y, 0)
            at = x + 1 - shift_x
            if key not in rows_made:
                value = table[channel[name], at]
                if shift_y > 0:
                    edge = jnp.broadcast_to(low_rows[rise.index(name), at], (SUB, LANE))
                    value = jnp.where(sub == 0, edge, pltpu.roll(value, 1, 0))
                elif shift_y < 0:
                    edge = jnp.broadcast_to(high_rows[fall.index(name), at], (SUB, LANE))
                    value = jnp.where(sub == SUB - 1, edge, pltpu.roll(value, SUB - 1, 0))
                rows_made[key] = value
            if shift_z == 0:
                return rows_made[key]
            deep = (name, shift_x, shift_y, shift_z)
            if deep not in rows_made:
                rows_made[deep] = lane_roll(rows_made[key], shift_z)
            return rows_made[deep]

        force = [jnp.zeros((SUB, LANE), jnp.float32) for compo in range(3)]
        for i in range(1, 19):
            shift = lattice_dirs[i]
            source = moved(i, *shift)
            rho = moved(19, *shift)
            fluid = rho > 0.0
            bounce = table[channel[opposite[i]], x + 1] + here_rho * source
            fresh = jnp.where(fluid, source, bounce)
            out_pops[i, x] = jnp.where(solid, pops[i, x], fresh)
            drag = rho * ((6.0 * lattice_weights[i]) * project(i, speeds))
            link = jnp.where(fluid, 2.0 * source - drag, 0.0)
            for compo in range(3):
                if shift[compo] > 0:
                    force[compo] = force[compo] + link
                elif shift[compo] < 0:
                    force[compo] = force[compo] - link
        force = [jnp.where(solid, part, 0.0) for part in force]
        where = split(cells[x])
        return total + sums_by_entry(force, *where)

    slot_force = lax.fori_loop(0, width, stream, jnp.zeros((32, LANE), jnp.float32))

    for place in range(per_row):
        value = jnp.zeros((SUB, LANE), jnp.float32)
        for compo in range(3):
            part = lane_roll(slot_force[compo * SUB : (compo + 1) * SUB], (compo - place) * slot)
            value = jnp.where(field == compo, part, value)
        sent_force[place, :, 0, :] = value
    everyone(
        lambda peer: sent_force.at[lax.rem(peer, per_row), peer // per_row],
        got_force.at[me],
        2,
    )

    for y in range(SUB):
        pair_ids[0, y : y + 1] = pairs[0:1, y * LANE : (y + 1) * LANE]
        pair_ids[1, y : y + 1] = pairs[1:2, y * LANE : (y + 1) * LANE]
    first = pair_ids[0]
    first_bank, first_spot = split(first)

    def from_owned(ref, compo):
        value = jnp.zeros((SUB, LANE), jnp.float32)
        for h in range(banks):
            part = lookup(ref[compo : compo + 1, h * LANE : (h + 1) * LANE], first_spot)
            value = jnp.where(first_bank == h, part, value)
        return value

    row, spot = split(pair_ids[1])

    def from_known(field_table):
        return from_table([field_table[r : r + 1] for r in range(SUB)], row, spot)

    arrived(got_force, recv_sems, 1)
    known[my_place, my_line] = reply[me]
    pos_table = []
    for compo in range(4):
        value = jnp.zeros((SUB, LANE), jnp.float32)
        for place in range(per_row):
            moved_lanes = lane_roll(known[place, :, 0, :], (place - compo) * slot)
            value = jnp.where(field == place, moved_lanes, value)
        pos_table.append(value)
    push = contact_push(
        [from_owned(position, compo) for compo in range(3)],
        [from_owned(velocity, compo) for compo in range(3)],
        from_owned(radius, 0),
        [from_known(pos_table[compo]) for compo in range(3)],
        [from_known(vel_table[compo]) for compo in range(3)],
        from_known(pos_table[3]),
    )
    contact = sums_by_entry(push, first_bank, first_spot)

    arrived(measure_vel, send_sems, 3)
    arrived(asked, send_sems, 0)
    arrived(reply, send_sems, 1)
    arrived(got_force, recv_sems, 2)
    got_force[me] = sent_force[my_place, my_line]
    gained = []
    for compo in range(3):
        value = jnp.zeros((SUB, LANE), jnp.float32)
        for q in range(groups):
            part = got_force[q * SUB : (q + 1) * SUB, 0, :]
            value = jnp.where(field == q, lane_roll(part, (q - compo) * slot), value)
        gained.append(value)
    fluid_force = sums_by_entry(gained, wanted_bank, wanted_spot)
    force = fluid_force + contact
    for compo in range(3):
        for h in range(banks):
            span = slice(h * LANE, (h + 1) * LANE)
            line = compo * SUB + h
            out_force[compo : compo + 1, span] = force[line : line + 1]
    arrived(got_force, send_sems, 2)


def local(
    populations,
    cell_grain,
    near_rows,
    contact_pairs,
    grain_position,
    grain_velocity,
    grain_radius,
    grain_mass,
):
    count_x = lax.axis_size("gx")
    count_y = lax.axis_size("yz")
    devices = count_x * count_y
    near_count = near_rows.shape[1]
    slot = near_count // devices
    owned = grain_position.shape[1]
    width = populations.shape[1]
    near_lines = near_rows.reshape(near_count // LANE, 1, LANE)
    whole = pl.BlockSpec(memory_space=pltpu.VMEM)
    f32 = jnp.float32
    assert slot & (slot - 1) == 0 and near_count == SUB * LANE
    lines = 3 * owned // LANE
    per_row = LANE // slot
    radius_line = grain_radius.reshape(1, owned)
    read, force = pl.pallas_call(
        functools.partial(kernel, count_x, count_y, slot),
        out_shape=(
            pltpu.VMEM(populations.shape, f32),
            jax.ShapeDtypeStruct(grain_velocity.shape, f32),
        ),
        in_specs=[pl.BlockSpec(memory_space=pltpu.HBM)] * 7,
        out_specs=(whole,) * 2,
        scratch_shapes=[
            pltpu.VMEM(populations.shape, f32),
            pltpu.VMEM(cell_grain.shape, jnp.int32),
            pltpu.VMEM(near_lines.shape, jnp.int32),
            pltpu.VMEM(contact_pairs.shape, jnp.int32),
            pltpu.VMEM(grain_position.shape, f32),
            pltpu.VMEM(grain_velocity.shape, f32),
            pltpu.VMEM(radius_line.shape, f32),
            pltpu.VMEM((lines, 1, LANE), f32),
            pltpu.VMEM((per_row, lines, SUB, 1, LANE), f32),
            pltpu.VMEM(((devices - 1) * lines, 1, LANE), f32),
            pltpu.VMEM((devices, 1, LANE), jnp.int32),
            pltpu.VMEM((devices, 1, LANE), f32),
            pltpu.VMEM((per_row, SUB, 1, LANE), f32),
            pltpu.VMEM((per_row, SUB, 1, LANE), f32),
            pltpu.VMEM((devices, 1, LANE), f32),
            pltpu.VMEM((CHANNELS, width + 2, SUB, LANE), f32),
            pltpu.VMEM((3, width, SUB, LANE), f32),
            pltpu.VMEM((FACE, width, 1, LANE), f32),
            pltpu.VMEM((FACE, width, 1, LANE), f32),
            pltpu.VMEM((FACE, width + 2, 1, LANE), f32),
            pltpu.VMEM((FACE, width + 2, 1, LANE), f32),
            pltpu.VMEM((2, SUB, LANE), jnp.int32),
            pltpu.SemaphoreType.DMA((4,)),
            pltpu.SemaphoreType.DMA((4,)),
            pltpu.SemaphoreType.DMA((8,)),
            pltpu.SemaphoreType.DMA((8,)),
            pltpu.SemaphoreType.DMA((7,)),
        ],
        compiler_params=pltpu.CompilerParams(
            collective_id=0, has_side_effects=True, vmem_limit_bytes=24 << 20
        ),
        name="step",
    )(
        *(
            pltpu.with_memory_space_constraint(array, pltpu.HBM)
            for array in (
                populations,
                cell_grain,
                near_lines,
                contact_pairs,
                grain_position,
                grain_velocity,
                radius_line,
            )
        )
    )
    velocity_next = grain_velocity + force / grain_mass[None]
    return read, velocity_next, grain_position + velocity_next


def solution(mesh):
    return jax.shard_map(
        local,
        mesh=mesh,
        in_specs=(
            P(None, "gx", "yz", None),
            P("gx", "yz", None),
            P(("gx", "yz"), None),
            P(None, ("gx", "yz")),
            P(None, ("gx", "yz")),
            P(None, ("gx", "yz")),
            P(("gx", "yz")),
            P(("gx", "yz")),
        ),
        out_specs=(P(None, "gx", "yz", None), P(None, ("gx", "yz")), P(None, ("gx", "yz"))),
        check_vma=False,
    )
```

```python
import functools

import jax
import jax.numpy as jnp
from jax import lax
from jax.experimental import pallas as pl
from jax.experimental.pallas import tpu as pltpu
from jax.sharding import PartitionSpec as P

lattice_dirs = (
    (0, 0, 0),
    (1, 0, 0),
    (-1, 0, 0),
    (0, 1, 0),
    (0, -1, 0),
    (0, 0, 1),
    (0, 0, -1),
    (1, 1, 0),
    (-1, -1, 0),
    (1, -1, 0),
    (-1, 1, 0),
    (1, 0, 1),
    (-1, 0, -1),
    (1, 0, -1),
    (-1, 0, 1),
    (0, 1, 1),
    (0, -1, -1),
    (0, 1, -1),
    (0, -1, 1),
)
lattice_weights = (1.0 / 3.0,) + (1.0 / 18.0,) * 6 + (1.0 / 36.0,) * 12
opposite = (0, 2, 1, 4, 3, 6, 5, 8, 7, 10, 9, 12, 11, 14, 13, 16, 15, 18, 17)
relax_rate = 1.25
stiffness = 0.5
damping = 0.5

still = (0, 3, 4, 5, 6, 15, 16, 17, 18)
ahead = (1, 7, 9, 11, 13)
behind = (2, 8, 10, 12, 14)
channel = {}
for place, name in enumerate(still + ahead):
    channel[name] = place
RHO = len(still) + len(ahead)
for place, name in enumerate(behind):
    channel[name] = RHO + 1 + place
CHANNELS = RHO + 1 + len(behind)
X_LOW = len(still)
rise = (3, 15, 17, 7, 19, 10)
fall = (4, 16, 18, 8, 19, 9)
channel[19] = RHO
FACE = 6
SUB = 8
LANE = 128


def project(direction, parts):
    total = None
    for compo in range(3):
        factor = lattice_dirs[direction][compo]
        if factor != 0:
            term = parts[compo] if factor > 0 else -parts[compo]
            total = term if total is None else total + term
    return total


def lookup(row, lanes):
    table = jnp.broadcast_to(row, lanes.shape)
    return jnp.take_along_axis(table, lanes, axis=1, mode="promise_in_bounds")


def split(ids):
    return lax.shift_right_arithmetic(ids, 7), jnp.bitwise_and(ids, LANE - 1)


def lane_roll(value, shift):
    shift = shift % LANE
    return value if shift == 0 else pltpu.roll(value, shift, 1)


def sums_by_entry(parts, rows, lanes):
    sub = lax.broadcasted_iota(jnp.int32, (SUB, LANE), 0)
    tall = lax.broadcasted_iota(jnp.int32, (LANE, LANE), 0)
    left = [[] for part in parts]
    right = []
    for y in range(SUB):
        hit = jnp.broadcast_to(rows[y : y + 1], (SUB, LANE)) == sub
        for which, part in enumerate(parts):
            spread = jnp.broadcast_to(part[y : y + 1], (SUB, LANE))
            left[which].append(jnp.where(hit, spread, 0.0))
        match = jnp.broadcast_to(lanes[y : y + 1], (LANE, LANE)) == tall
        right.append(jnp.where(match, 1.0, 0.0).astype(jnp.bfloat16))
    wide = [jnp.concatenate(pieces, axis=1) for pieces in left]
    wide.append(jnp.zeros_like(wide[0]))
    full = jnp.concatenate(wide, axis=0)
    first = full.astype(jnp.bfloat16)
    rest = full - first.astype(jnp.float32)
    second = rest.astype(jnp.bfloat16)
    third = (rest - second.astype(jnp.float32)).astype(jnp.bfloat16)
    table = jnp.concatenate(right, axis=1)
    total = lax.dot_general(
        jnp.concatenate([first, second, third], axis=0),
        table,
        (((1,), (1,)), ((), ())),
        preferred_element_type=jnp.float32,
    )
    return total[0:32] + total[32:64] + total[64:96]


def contact_push(pos_a, vel_a, rad_a, pos_b, vel_b, rad_b):
    offset = [a - b for a, b in zip(pos_a, pos_b)]
    length = jnp.sqrt(offset[0] * offset[0] + offset[1] * offset[1] + offset[2] * offset[2])
    scale = jnp.maximum(length, 1.0)
    normal = [part / scale for part in offset]
    intersection = jnp.maximum(rad_a + rad_b - length, 0.0)
    closing = (
        (vel_a[0] - vel_b[0]) * normal[0]
        + (vel_a[1] - vel_b[1]) * normal[1]
        + (vel_a[2] - vel_b[2]) * normal[2]
    )
    amount = stiffness * intersection - damping * intersection * closing
    return [amount * part for part in normal]


def kernel(
    count_x,
    count_y,
    slot,
    pops_in,
    cells_in,
    near_in,
    pairs_in,
    position_in,
    velocity_in,
    radius_in,
    out_pops,
    out_force,
    pops,
    cells,
    near,
    pairs,
    position,
    velocity,
    radius,
    vel_lines,
    all_vel,
    measure_vel,
    asked,
    reply,
    known,
    sent_force,
    got_force,
    table,
    wall,
    low_src,
    high_src,
    low_rows,
    high_rows,
    pair_ids,
    send_sems,
    recv_sems,
    halo_send,
    halo_recv,
    load_sems,
):
    devices = count_x * count_y
    groups = devices // SUB
    per_row = LANE // slot
    width = pops.shape[1]
    owned = position.shape[1]
    banks = owned // LANE
    at_x = lax.axis_index("gx")
    at_y = lax.axis_index("yz")
    me = at_x * count_y + at_y
    sub = lax.broadcasted_iota(jnp.int32, (SUB, LANE), 0)
    lane = lax.broadcasted_iota(jnp.int32, (SUB, LANE), 1)

    offsets = [
        (step_x, step_y)
        for step_x in sorted(range(count_x), key=lambda step: abs(2 * step - count_x))
        for step_y in reversed(range(count_y))
        if step_x or step_y
    ]
    line_x = [lax.rem(at_x + step, count_x) for step in range(count_x)]
    line_y = [lax.rem(at_y + step, count_y) for step in range(count_y)]

    barrier = pltpu.get_barrier_semaphore()
    for step_x, step_y in offsets:
        pl.semaphore_signal(
            barrier,
            inc=1,
            device_id=(line_x[step_x], line_y[step_y]),
            device_id_type=pl.DeviceIdType.MESH,
        )
    loads = []
    for place, (source, target) in enumerate(
        (
            (near_in, near),
            (velocity_in, velocity),
            (position_in, position),
            (radius_in, radius),
            (pops_in, pops),
            (cells_in, cells),
            (pairs_in, pairs),
        )
    ):
        load = pltpu.make_async_copy(source, target, load_sems.at[place])
        load.start()
        loads.append(load)
    my_line = me // per_row
    my_place = lax.rem(me, per_row)
    loads[1].wait()
    for compo in range(3):
        for h in range(banks):
            line = velocity[compo : compo + 1, h * LANE : (h + 1) * LANE]
            vel_lines[compo * banks + h] = line
            all_vel[my_place, compo * banks + h, my_line] = line
    loads[0].wait()
    asked[pl.ds(me, 1)] = near[pl.ds(me // per_row, 1)]
    pl.semaphore_wait(barrier, devices - 1)

    def everyone(source_of, target_at_me, which):
        for step_x, step_y in offsets:
            to_x, to_y = line_x[step_x], line_y[step_y]
            pltpu.make_async_remote_copy(
                src_ref=source_of(to_x * count_y + to_y),
                dst_ref=target_at_me,
                send_sem=send_sems.at[which],
                recv_sem=recv_sems.at[which],
                device_id=(to_x, to_y),
                device_id_type=pl.DeviceIdType.MESH,
            ).start()

    def arrived(target, sems, which):
        part = target if target is measure_vel else target.at[pl.ds(0, devices - 1)]
        pltpu.make_async_copy(part, part, sems.at[which]).wait()

    everyone(lambda peer: vel_lines, all_vel.at[my_place, :, my_line], 3)
    everyone(lambda peer: near.at[peer // per_row], asked.at[me], 0)
    for load in loads[2:]:
        load.wait()

    def collide(x, carry):
        values = [pops[i, x] for i in range(19)]
        density = values[0]
        for i in range(1, 19):
            density = density + values[i]
        scale = 1.0 / density
        speeds = []
        for compo in range(3):
            moment = None
            for i in range(19):
                factor = lattice_dirs[i][compo]
                if factor != 0:
                    if moment is None:
                        moment = values[i]
                    elif factor > 0:
                        moment = moment + values[i]
                    else:
                        moment = moment - values[i]
            speeds.append(moment * scale)
        square = speeds[0] * speeds[0] + speeds[1] * speeds[1] + speeds[2] * speeds[2]
        base = 1.0 - 1.5 * square
        weighted = {w: (relax_rate * w) * density for w in set(lattice_weights)}
        keep = 1.0 - relax_rate
        fresh = keep * values[0] + weighted[lattice_weights[0]] * base
        table[channel[0], x + 1] = fresh
        after = fresh
        for i in range(1, 19, 2):
            along = project(i, speeds)
            even = base + 4.5 * along * along
            odd = 3.0 * along
            gain = weighted[lattice_weights[i]]
            plus = keep * values[i] + gain * (even + odd)
            minus = keep * values[i + 1] + gain * (even - odd)
            table[channel[i], x + 1] = plus
            table[channel[i + 1], x + 1] = minus
            after = after + plus + minus
        table[RHO, x + 1] = jnp.where(cells[x] >= 0, 0.0, after)
        return carry

    lax.fori_loop(0, width, collide, 0)

    slot_bits = slot.bit_length() - 1
    field = lax.shift_right_logical(lane, slot_bits)
    near_bank, near_spot = split(
        jnp.concatenate([near[line] for line in range(SUB)], axis=0)
    )
    arrived(measure_vel, recv_sems, 3)
    vel_table = [jnp.zeros((SUB, LANE), jnp.float32) for compo in range(3)]
    for place in range(per_row):
        for h in range(banks):
            mine = (field == place) & (near_bank == h)
            for compo in range(3):
                lines = all_vel[place, compo * banks + h, :, 0, :]
                part = jnp.take_along_axis(
                    lines, near_spot, axis=1, mode="promise_in_bounds"
                )
                vel_table[compo] = jnp.where(mine, part, vel_table[compo])
    vel_rows = [[part[r : r + 1] for r in range(SUB)] for part in vel_table]

    def from_table(rows_of, row, spot):
        value = jnp.zeros((SUB, LANE), jnp.float32)
        for r in range(SUB):
            value = jnp.where(row == r, lookup(rows_of[r], spot), value)
        return value

    def fill_walls(x, carry):
        ids = cells[x]
        solid = ids >= 0
        row, spot = split(ids)
        speeds = [from_table(rows_of, row, spot) for rows_of in vel_rows]
        for compo in range(3):
            wall[compo, x] = speeds[compo]
        for i in range(1, 19, 2):
            motion = (6.0 * lattice_weights[i]) * project(i, speeds)
            plus = jnp.where(solid, motion, table[channel[i], x + 1])
            minus = jnp.where(solid, -motion, table[channel[i + 1], x + 1])
            table[channel[i], x + 1] = plus
            table[channel[i + 1], x + 1] = minus
            for which, value in ((i, plus), (i + 1, minus)):
                if which in rise:
                    high_src[rise.index(which), pl.ds(x, 1)] = value[SUB - 1 : SUB][None]
                if which in fall:
                    low_src[fall.index(which), pl.ds(x, 1)] = value[0:1][None]
        rho = table[RHO, x + 1]
        high_src[4, pl.ds(x, 1)] = rho[SUB - 1 : SUB][None]
        low_src[4, pl.ds(x, 1)] = rho[0:1][None]
        return carry

    lax.fori_loop(0, width, fill_walls, 0, unroll=4)

    right = lax.rem(at_x + 1, count_x)
    left = lax.rem(at_x + count_x - 1, count_x)
    upper = lax.rem(at_y + 1, count_y)
    lower = lax.rem(at_y + count_y - 1, count_y)
    end = width - 1
    hops = (
        (table.at[X_LOW : X_LOW + FACE, width], table.at[X_LOW : X_LOW + FACE, 0], right, at_y),
        (table.at[RHO : RHO + FACE, 1], table.at[RHO : RHO + FACE, width + 1], left, at_y),
        (high_src, low_rows.at[:, 1 : width + 1], at_x, upper),
        (low_src, high_rows.at[:, 1 : width + 1], at_x, lower),
        (high_src.at[3:5, end], low_rows.at[3:5, 0], right, upper),
        (high_src.at[4:6, 0], low_rows.at[4:6, width + 1], left, upper),
        (low_src.at[3:5, 0], high_rows.at[3:5, width + 1], left, lower),
        (low_src.at[4:6, end], high_rows.at[4:6, 0], right, lower),
    )
    copies = []
    for which, (source, target, to_x, to_y) in enumerate(hops):
        copy = pltpu.make_async_remote_copy(
            src_ref=source,
            dst_ref=target,
            send_sem=halo_send.at[which],
            recv_sem=halo_recv.at[which],
            device_id=(to_x, to_y),
            device_id_type=pl.DeviceIdType.MESH,
        )
        copy.start()
        copies.append(copy)

    arrived(asked, recv_sems, 0)
    quarter = my_place
    within = jnp.bitwise_and(lane, slot - 1)
    wanted = []
    for q in range(groups):
        ask = asked[q * SUB : (q + 1) * SUB, 0, :]
        row = jnp.take_along_axis(
            ask, within + quarter * slot, axis=1, mode="promise_in_bounds"
        )
        wanted.append(row)
        bank, spot = split(jnp.maximum(row, 0))
        pos_row = jnp.zeros((SUB, LANE), jnp.float32)
        for h in range(banks):
            span = slice(h * LANE, (h + 1) * LANE)
            for compo in range(4):
                source = radius[0:1, span] if compo == 3 else position[compo : compo + 1, span]
                mine = (bank == h) & (field == compo)
                pos_row = jnp.where(mine, lookup(source, spot), pos_row)
        reply[q * SUB : (q + 1) * SUB, 0, :] = pos_row
    everyone(lambda peer: reply.at[peer], known.at[my_place, my_line], 1)

    wanted_table = jnp.zeros((SUB, LANE), jnp.int32)
    for q in range(groups):
        wanted_table = jnp.where(field == q, lane_roll(wanted[q], q * slot), wanted_table)
    wanted_bank, wanted_spot = split(wanted_table)

    for copy in copies:
        copy.wait()

    def stream(x, total):
        solid = cells[x] >= 0
        here_rho = table[RHO, x + 1]
        speeds = [wall[compo, x] for compo in range(3)]
        out_pops[0, x] = jnp.where(solid, pops[0, x], table[channel[0], x + 1])
        rows_made = {}

        def moved(name, shift_x, shift_y, shift_z):
            key = (name, shift_x, shift_y, 0)
            at = x + 1 - shift_x
            if key not in rows_made:
                value = table[channel[name], at]
                if shift_y > 0:
                    edge = jnp.broadcast_to(low_rows[rise.index(name), at], (SUB, LANE))
                    value = jnp.where(sub == 0, edge, pltpu.roll(value, 1, 0))
                elif shift_y < 0:
                    edge = jnp.broadcast_to(high_rows[fall.index(name), at], (SUB, LANE))
                    value = jnp.where(sub == SUB - 1, edge, pltpu.roll(value, SUB - 1, 0))
                rows_made[key] = value
            if shift_z == 0:
                return rows_made[key]
            deep = (name, shift_x, shift_y, shift_z)
            if deep not in rows_made:
                rows_made[deep] = lane_roll(rows_made[key], shift_z)
            return rows_made[deep]

        force = [jnp.zeros((SUB, LANE), jnp.float32) for compo in range(3)]
        for i in range(1, 19):
            shift = lattice_dirs[i]
            source = moved(i, *shift)
            rho = moved(19, *shift)
            fluid = rho > 0.0
            bounce = table[channel[opposite[i]], x + 1] + here_rho * source
            fresh = jnp.where(fluid, source, bounce)
            out_pops[i, x] = jnp.where(solid, pops[i, x], fresh)
            drag = rho * ((6.0 * lattice_weights[i]) * project(i, speeds))
            link = jnp.where(fluid, 2.0 * source - drag, 0.0)
            for compo in range(3):
                if shift[compo] > 0:
                    force[compo] = force[compo] + link
                elif shift[compo] < 0:
                    force[compo] = force[compo] - link
        force = [jnp.where(solid, part, 0.0) for part in force]
        where = split(cells[x])
        return total + sums_by_entry(force, *where)

    slot_force = lax.fori_loop(0, width, stream, jnp.zeros((32, LANE), jnp.float32), unroll=4)

    for place in range(per_row):
        value = jnp.zeros((SUB, LANE), jnp.float32)
        for compo in range(3):
            part = lane_roll(slot_force[compo * SUB : (compo + 1) * SUB], (compo - place) * slot)
            value = jnp.where(field == compo, part, value)
        sent_force[place, :, 0, :] = value
    everyone(
        lambda peer: sent_force.at[lax.rem(peer, per_row), peer // per_row],
        got_force.at[me],
        2,
    )

    for y in range(SUB):
        pair_ids[0, y : y + 1] = pairs[0:1, y * LANE : (y + 1) * LANE]
        pair_ids[1, y : y + 1] = pairs[1:2, y * LANE : (y + 1) * LANE]
    first = pair_ids[0]
    first_bank, first_spot = split(first)

    def from_owned(ref, compo):
        value = jnp.zeros((SUB, LANE), jnp.float32)
        for h in range(banks):
            part = lookup(ref[compo : compo + 1, h * LANE : (h + 1) * LANE], first_spot)
            value = jnp.where(first_bank == h, part, value)
        return value

    row, spot = split(pair_ids[1])

    def from_known(field_table):
        return from_table([field_table[r : r + 1] for r in range(SUB)], row, spot)

    arrived(got_force, recv_sems, 1)
    known[my_place, my_line] = reply[me]
    pos_table = []
    for compo in range(4):
        value = jnp.zeros((SUB, LANE), jnp.float32)
        for place in range(per_row):
            moved_lanes = lane_roll(known[place, :, 0, :], (place - compo) * slot)
            value = jnp.where(field == place, moved_lanes, value)
        pos_table.append(value)
    push = contact_push(
        [from_owned(position, compo) for compo in range(3)],
        [from_owned(velocity, compo) for compo in range(3)],
        from_owned(radius, 0),
        [from_known(pos_table[compo]) for compo in range(3)],
        [from_known(vel_table[compo]) for compo in range(3)],
        from_known(pos_table[3]),
    )
    contact = sums_by_entry(push, first_bank, first_spot)

    arrived(measure_vel, send_sems, 3)
    arrived(asked, send_sems, 0)
    arrived(reply, send_sems, 1)
    arrived(got_force, recv_sems, 2)
    got_force[me] = sent_force[my_place, my_line]
    gained = []
    for compo in range(3):
        value = jnp.zeros((SUB, LANE), jnp.float32)
        for q in range(groups):
            part = got_force[q * SUB : (q + 1) * SUB, 0, :]
            value = jnp.where(field == q, lane_roll(part, (q - compo) * slot), value)
        gained.append(value)
    fluid_force = sums_by_entry(gained, wanted_bank, wanted_spot)
    force = fluid_force + contact
    for compo in range(3):
        for h in range(banks):
            span = slice(h * LANE, (h + 1) * LANE)
            line = compo * SUB + h
            out_force[compo : compo + 1, span] = force[line : line + 1]
    arrived(got_force, send_sems, 2)


def local(
    populations,
    cell_grain,
    near_rows,
    contact_pairs,
    grain_position,
    grain_velocity,
    grain_radius,
    grain_mass,
):
    count_x = lax.axis_size("gx")
    count_y = lax.axis_size("yz")
    devices = count_x * count_y
    near_count = near_rows.shape[1]
    slot = near_count // devices
    owned = grain_position.shape[1]
    width = populations.shape[1]
    near_lines = near_rows.reshape(near_count // LANE, 1, LANE)
    whole = pl.BlockSpec(memory_space=pltpu.VMEM)
    f32 = jnp.float32
    assert slot & (slot - 1) == 0 and near_count == SUB * LANE
    lines = 3 * owned // LANE
    per_row = LANE // slot
    radius_line = grain_radius.reshape(1, owned)
    read, force = pl.pallas_call(
        functools.partial(kernel, count_x, count_y, slot),
        out_shape=(
            pltpu.VMEM(populations.shape, f32),
            jax.ShapeDtypeStruct(grain_velocity.shape, f32),
        ),
        in_specs=[pl.BlockSpec(memory_space=pltpu.HBM)] * 7,
        out_specs=(whole,) * 2,
        scratch_shapes=[
            pltpu.VMEM(populations.shape, f32),
            pltpu.VMEM(cell_grain.shape, jnp.int32),
            pltpu.VMEM(near_lines.shape, jnp.int32),
            pltpu.VMEM(contact_pairs.shape, jnp.int32),
            pltpu.VMEM(grain_position.shape, f32),
            pltpu.VMEM(grain_velocity.shape, f32),
            pltpu.VMEM(radius_line.shape, f32),
            pltpu.VMEM((lines, 1, LANE), f32),
            pltpu.VMEM((per_row, lines, SUB, 1, LANE), f32),
            pltpu.VMEM(((devices - 1) * lines, 1, LANE), f32),
            pltpu.VMEM((devices, 1, LANE), jnp.int32),
            pltpu.VMEM((devices, 1, LANE), f32),
            pltpu.VMEM((per_row, SUB, 1, LANE), f32),
            pltpu.VMEM((per_row, SUB, 1, LANE), f32),
            pltpu.VMEM((devices, 1, LANE), f32),
            pltpu.VMEM((CHANNELS, width + 2, SUB, LANE), f32),
            pltpu.VMEM((3, width, SUB, LANE), f32),
            pltpu.VMEM((FACE, width, 1, LANE), f32),
            pltpu.VMEM((FACE, width, 1, LANE), f32),
            pltpu.VMEM((FACE, width + 2, 1, LANE), f32),
            pltpu.VMEM((FACE, width + 2, 1, LANE), f32),
            pltpu.VMEM((2, SUB, LANE), jnp.int32),
            pltpu.SemaphoreType.DMA((4,)),
            pltpu.SemaphoreType.DMA((4,)),
            pltpu.SemaphoreType.DMA((8,)),
            pltpu.SemaphoreType.DMA((8,)),
            pltpu.SemaphoreType.DMA((7,)),
        ],
        compiler_params=pltpu.CompilerParams(
            collective_id=0, has_side_effects=True, vmem_limit_bytes=24 << 20
        ),
        name="step",
    )(
        *(
            pltpu.with_memory_space_constraint(array, pltpu.HBM)
            for array in (
                populations,
                cell_grain,
                near_lines,
                contact_pairs,
                grain_position,
                grain_velocity,
                radius_line,
            )
        )
    )
    velocity_next = grain_velocity + force / grain_mass[None]
    return read, velocity_next, grain_position + velocity_next


def solution(mesh):
    return jax.shard_map(
        local,
        mesh=mesh,
        in_specs=(
            P(None, "gx", "yz", None),
            P("gx", "yz", None),
            P(("gx", "yz"), None),
            P(None, ("gx", "yz")),
            P(None, ("gx", "yz")),
            P(None, ("gx", "yz")),
            P(("gx", "yz")),
            P(("gx", "yz")),
        ),
        out_specs=(P(None, "gx", "yz", None), P(None, ("gx", "yz")), P(None, ("gx", "yz"))),
        check_vma=False,
    )
```
